128 devices in a mesh: ctx: 16 (over x_lo, y, core), head: 8 (over x_hi, z).
Axes of the slice: x: 4 (x_hi: 2, x_lo: 2; x = x_hi * 2 + x_lo), y: 4, z: 4, core: 2. Of those that a mesh axis runs over, the one named last changes fastest.
Arguments:
- q_latent: bfloat16 [4096, 1536], P('ctx', 'head'), may hold values from -70 to 70
- kv_latent: bfloat16 [4096, 576], P('ctx', 'head'), may hold values from -6 to 6
- w_query: bfloat16 [1536, 24576], P(None, 'head'), may hold values from -0.15625 to 0.15625
- w_key: bfloat16 [512, 16384], P(None, 'head'), may hold values from -0.25 to 0.25
- w_value: bfloat16 [512, 16384], P(None, 'head'), may hold values from -0.25 to 0.25
- d_out: bfloat16 [4096, 16384], P('ctx', 'head'), may hold values from -6 to 6
Outputs:
- attn_out: bfloat16 [4096, 16384], P('ctx', 'head')
- grad_qlat: float32 [4096, 1536], P('ctx', 'head')
- grad_kvlat: float32 [4096, 576], P('ctx', 'head')
The draws below stay inside these ranges and needn't reach their ends.
All inputs are finite; a program needn't handle non-finite values.
Results may differ from the reference program's by a relative error of at most 0.023.
The reference program's roundings to bfloat16 on the way (of `queries`, `probs_b`, `dscore` and `grad_query`) count: a program that leaves them out, or rounds other values in their place, can miss the bound.
Values may be sent and summed in bfloat16 or wider, within the bound.
No kernel may reach another device: no remote copies, remote signals or barrier semaphores. Data moves between devices by JAX's collectives and lax.ppermute only.
A program may use at most 128 MiB of HBM per device.

```python
import jax
import jax.numpy as jnp
from jax import lax

QL = 1536
KVL = 512
ROPE = 64
NOPE = 128
VDIM = 128
HEAD_DEV = 16
TOK_DEV = 256
HEADS = 128
TOKENS = 4096
N_CTX = 16
N_HEAD = 8


def draw_q_latent(key, part):
    base_key = jax.random.fold_in(jax.random.fold_in(key, 11), 0)
    values = jax.random.normal(base_key, (TOKENS, QL), jnp.float32)
    return jnp.clip(values, -6.0, 6.0).astype(jnp.bfloat16)


def steps_of(key, dims, shards, low, high):
    def one(axis_at, parts):
        heights = jax.random.uniform(jax.random.fold_in(jax.random.fold_in(key, 6), axis_at), (parts,), jnp.float32, low / len(shards), high / len(shards))
        return jnp.repeat(jnp.exp(heights), dims[axis_at] // parts).reshape((-1,) + (1,) * (len(dims) - axis_at - 1))

    factor_of = one(*shards[0])
    for cut in shards[1:]:
        factor_of = factor_of * one(*cut)
    return factor_of


def noise(stream_key, dims, deviation, reach, cuts=(), held_as=jnp.bfloat16):
    loudness = steps_of(stream_key, dims, cuts, -0.22, 0.18) if cuts else 1.0
    result = jax.random.normal(stream_key, dims, jnp.float32) * deviation * loudness
    return jnp.minimum(jnp.maximum(result, -reach), reach).astype(held_as)


def setup_inputs(seed: int = 0) -> dict:
    streams_of = jax.random.split(jax.random.key(seed), 7)
    return {
        "q_latent": draw_q_latent(jax.random.fold_in(streams_of[6], 71), 0),
        "kv_latent": noise(streams_of[1], (TOKENS, KVL + ROPE), 1.0, 6.0, ((0, 16), (1, 8))),
        "w_query": noise(streams_of[2], (QL, HEADS * (NOPE + ROPE)), QL ** -0.5, 0.15625, ((1, 8),)),
        "w_key": noise(streams_of[3], (KVL, HEADS * NOPE), KVL ** -0.5, 0.25, ((1, 8),)),
        "w_value": noise(streams_of[4], (KVL, HEADS * VDIM), KVL ** -0.5, 0.25, ((1, 8),)),
        "d_out": noise(streams_of[5], (TOKENS, HEADS * VDIM), 1.0, 6.0, ((0, 16), (1, 8))),
    }


def to_float(array):
    return array.astype(jnp.float32)


def shift_down(array):
    return jnp.concatenate([jnp.zeros_like(array[:1]), array[:-1]], 0)


def shift_up(array):
    return jnp.concatenate([array[1:], jnp.zeros_like(array[:1])], 0)


def reference(q_latent, kv_latent, w_query, w_key, w_value, d_out):
    group_count = N_HEAD
    per_group = HEAD_DEV
    block_count = N_CTX
    block_rows = TOK_DEV
    width = NOPE + ROPE
    softmax_scale = width ** -0.5
    query_w = w_query.reshape(QL, group_count, per_group * width).transpose(1, 0, 2)
    key_w = w_key.reshape(KVL, group_count, per_group * NOPE).transpose(1, 0, 2)
    value_w = w_value.reshape(KVL, group_count, per_group * VDIM).transpose(1, 0, 2)
    grad_groups = d_out.reshape(TOKENS, group_count, per_group * VDIM).transpose(1, 0, 2)
    rope_keys = kv_latent[:, KVL:].reshape(block_count, block_rows, ROPE)
    rope_all = jnp.concatenate([shift_down(rope_keys), rope_keys], 1)
    query_pos = jnp.arange(block_rows)[:, None]
    key_pos = jnp.arange(2 * block_rows)[None, :]
    block_idx = jnp.arange(block_count)[:, None, None]
    visible = jnp.where(key_pos < block_rows, block_idx > 0, key_pos - block_rows <= query_pos)
    latent_main = kv_latent[:, :KVL]

    def group_step(carry, inputs):
        wq_group, wk_group, wv_group, grad_group = inputs
        queries = jnp.dot(q_latent, wq_group, preferred_element_type=jnp.float32).astype(jnp.bfloat16)
        queries = queries.reshape(block_count, block_rows, per_group, width)
        keys_nope = jnp.dot(latent_main, wk_group, preferred_element_type=jnp.float32).astype(jnp.bfloat16)
        keys_nope = keys_nope.reshape(block_count, block_rows, per_group, NOPE)
        values = jnp.dot(latent_main, wv_group, preferred_element_type=jnp.float32).astype(jnp.bfloat16)
        values = values.reshape(block_count, block_rows, per_group, VDIM)
        keys_all = jnp.concatenate([shift_down(keys_nope), keys_nope], 1)
        values_all = jnp.concatenate([shift_down(values), values], 1)
        query_nope = queries[..., :NOPE]
        query_rope = queries[..., NOPE:]
        scores = jnp.einsum("nqhd,nkhd->nhqk", to_float(query_nope), to_float(keys_all))
        scores = (scores + jnp.einsum("nqhr,nkr->nhqk", to_float(query_rope), to_float(rope_all))) * softmax_scale
        mask = visible[:, None]
        scores = jnp.where(mask, scores, jnp.float32(-1e30))
        maxima = jnp.max(scores, -1, keepdims=True)
        expons = jnp.where(mask, jnp.exp(scores - maxima), jnp.float32(0.0))
        probs = expons / jnp.sum(expons, -1, keepdims=True)
        probs_b = probs.astype(jnp.bfloat16)
        output = jnp.einsum("nhqk,nkhd->nqhd", to_float(probs_b), to_float(values_all)).astype(jnp.bfloat16)
        grad_out = grad_group.reshape(block_count, block_rows, per_group, VDIM)
        dprob = jnp.einsum("nqhd,nkhd->nhqk", to_float(grad_out), to_float(values_all))
        row_dot = jnp.sum(to_float(grad_out) * to_float(output), -1).transpose(0, 2, 1)[..., None]
        dscore = (probs * (dprob - row_dot) * softmax_scale).astype(jnp.bfloat16)
        grad_qnope = jnp.einsum("nhqk,nkhd->nqhd", to_float(dscore), to_float(keys_all))
        grad_qrope = jnp.einsum("nhqk,nkr->nqhr", to_float(dscore), to_float(rope_all))
        grad_query = jnp.concatenate([grad_qnope, grad_qrope], -1).astype(jnp.bfloat16)
        grad_query = grad_query.reshape(TOKENS, per_group * width)
        grad_qgroup = jnp.dot(grad_query, wq_group.T, preferred_element_type=jnp.float32)
        grad_knope = jnp.einsum("nhqk,nqhd->nkhd", to_float(dscore), to_float(query_nope)).astype(jnp.bfloat16)
        grad_krope = jnp.einsum("nhqk,nqhr->nkhr", to_float(dscore), to_float(query_rope)).astype(jnp.bfloat16)
        grad_value = jnp.einsum("nhqk,nqhd->nkhd", to_float(probs_b), to_float(grad_out)).astype(jnp.bfloat16)

        def project(knope_part, krope_part, value_part):
            main_cols = jnp.dot(knope_part.reshape(TOKENS, per_group * NOPE), wk_group.T, preferred_element_type=jnp.float32)
            main_cols = main_cols + jnp.dot(value_part.reshape(TOKENS, per_group * VDIM), wv_group.T, preferred_element_type=jnp.float32)
            rope_cols = jnp.sum(to_float(krope_part), axis=2).reshape(TOKENS, ROPE)
            return jnp.concatenate([main_cols, rope_cols], -1)

        own_part = project(grad_knope[:, block_rows:], grad_krope[:, block_rows:], grad_value[:, block_rows:])
        next_part = project(shift_up(grad_knope[:, :block_rows]), shift_up(grad_krope[:, :block_rows]), shift_up(grad_value[:, :block_rows]))
        carry = (carry[0] + grad_qgroup, carry[1] + own_part + next_part)
        return carry, output.reshape(TOKENS, per_group * VDIM)

    start = (jnp.zeros((TOKENS, QL), jnp.float32), jnp.zeros((TOKENS, KVL + ROPE), jnp.float32))
    grads, outputs = lax.scan(group_step, start, (query_w, key_w, value_w, grad_groups))
    attn_out = outputs.transpose(1, 0, 2).reshape(TOKENS, HEADS * VDIM)
    return attn_out, grads[0], grads[1]
```

```python
import math

import jax
import jax.numpy as jnp
from jax import lax
from jax.experimental import pallas as pl
from jax.experimental.pallas import tpu as pltpu
from jax.sharding import PartitionSpec as P

QL = 1536
KVL = 512
ROPE = 64
NOPE = 128
VDIM = 128
WIDTH = NOPE + ROPE
PAD = 256
HEAD_DEV = 16
TOK = 256
SCALE = WIDTH ** (-0.5)
LOG2E = 1.0 / math.log(2.0)
VMEM_LIMIT = 48 * 1024 * 1024

NN = (((1,), (0,)), ((), ()))
NT = (((1,), (1,)), ((), ()))


def mm(a, b, dims=NN):
    return lax.dot_general(a, b, dims, preferred_element_type=jnp.float32)


def params():
    return pltpu.CompilerParams(vmem_limit_bytes=VMEM_LIMIT)


P_HEADS = 4


def project_kernel(g_ref, kvt_ref, wq_ref, wk_ref, wv_ref, wkt_ref, wvt_ref,
                   q_ref, k_ref, v_ref, kt_ref, vt_ref, qlat, kv):
    @pl.when(pl.program_id(0) == 0)
    def _():
        rows = g_ref[:, : QL // 8, :].reshape(QL, TOK)
        for i in range(QL // 256):
            qlat[:, i * 256 : (i + 1) * 256] = rows[i * 256 : (i + 1) * 256].T
        for i in range(KVL // 256):
            kv[:, i * 256 : (i + 1) * 256] = kvt_ref[i * 256 : (i + 1) * 256, :].T

    queries = mm(qlat[...], wq_ref[...]).astype(jnp.bfloat16)
    zeros = jnp.zeros((TOK, PAD - WIDTH), jnp.bfloat16)
    for h in range(P_HEADS):
        q_ref[:, h * PAD : (h + 1) * PAD] = jnp.concatenate(
            [queries[:, h * WIDTH : (h + 1) * WIDTH], zeros], 1
        )
    k_ref[...] = mm(kv[...], wk_ref[...]).astype(jnp.bfloat16)
    v_ref[...] = mm(kv[...], wv_ref[...]).astype(jnp.bfloat16)
    main = kvt_ref[:KVL, :]
    kt_ref[...] = mm(wkt_ref[...], main).astype(jnp.bfloat16)
    vt_ref[...] = mm(wvt_ref[...], main).astype(jnp.bfloat16)


def project(g, kvt, wq, wk, wv, wkt, wvt):
    n = HEAD_DEV // P_HEADS
    cols = P_HEADS * NOPE
    whole = lambda *shape: pl.BlockSpec(shape, lambda i: (0,) * len(shape))
    shape = jax.ShapeDtypeStruct
    return pl.pallas_call(
        project_kernel,
        grid=(n,),
        in_specs=[
            whole(8, (QL + KVL + ROPE) // 8, TOK),
            whole(KVL + ROPE, TOK),
            pl.BlockSpec((QL, P_HEADS * WIDTH), lambda i: (0, i)),
            pl.BlockSpec((KVL, cols), lambda i: (0, i)),
            pl.BlockSpec((KVL, cols), lambda i: (0, i)),
            pl.BlockSpec((cols, KVL), lambda i: (i, 0)),
            pl.BlockSpec((cols, KVL), lambda i: (i, 0)),
        ],
        out_specs=[
            pl.BlockSpec((TOK, P_HEADS * PAD), lambda i: (0, i)),
            pl.BlockSpec((TOK, cols), lambda i: (0, i)),
            pl.BlockSpec((TOK, cols), lambda i: (0, i)),
            pl.BlockSpec((cols, TOK), lambda i: (i, 0)),
            pl.BlockSpec((cols, TOK), lambda i: (i, 0)),
        ],
        out_shape=[
            shape((TOK, HEAD_DEV * PAD), jnp.bfloat16),
            shape((TOK, HEAD_DEV * NOPE), jnp.bfloat16),
            shape((TOK, HEAD_DEV * VDIM), jnp.bfloat16),
            shape((HEAD_DEV * NOPE, TOK), jnp.bfloat16),
            shape((HEAD_DEV * VDIM, TOK), jnp.bfloat16),
        ],
        scratch_shapes=[
            pltpu.VMEM((TOK, QL), jnp.bfloat16),
            pltpu.VMEM((TOK, KVL), jnp.bfloat16),
        ],
        compiler_params=params(),
        name="project",
    )(g, kvt, wq, wk, wv, wkt, wvt)


A_HEADS = 2


def attend_kernel(lead_ref, kvt_ref, pkvt_ref, q_ref, k_ref, v_ref, kt_ref, vt_ref,
                  dot_ref, wk_ref, wv_ref, wkt_ref, wvt_ref,
                  ot_ref, dqt_ref, dk_ref, dv_ref, early_ref, own_rope_ref,
                  bias, pkv, kx, vx, ktx, vtx, dkp, dvp, acc, rope):
    step = pl.program_id(0)

    @pl.when(step == 0)
    def _():
        key = lax.broadcasted_iota(jnp.int32, (2 * TOK, TOK), 0)
        query = lax.broadcasted_iota(jnp.int32, (2 * TOK, TOK), 1)
        hidden = jnp.where(key < TOK, jnp.where(lead_ref[0] > 0, key + TOK, key - TOK), key - TOK - query)
        bias[...] = jnp.where(hidden > 0, jnp.float32(-1e30), jnp.float32(0.0))
        for i in range(KVL // 256):
            pkv[:, i * 256 : (i + 1) * 256] = pkvt_ref[i * 256 : (i + 1) * 256, :].T
        ropes_t = jnp.concatenate([pkvt_ref[KVL:, :], kvt_ref[KVL:, :]], 1)
        padded = jnp.concatenate([ropes_t, jnp.zeros_like(ropes_t)], 0)
        ropes = padded.T
        for h in range(A_HEADS):
            kx[h, :, NOPE:] = ropes
            ktx[h, NOPE:, :] = ropes_t
        acc[...] = jnp.zeros_like(acc)
        rope[...] = jnp.zeros_like(rope)

    main = pkvt_ref[:KVL, :]
    keys = mm(pkv[...], wk_ref[...]).astype(jnp.bfloat16)
    vals = mm(pkv[...], wv_ref[...]).astype(jnp.bfloat16)
    keys_t = mm(wkt_ref[...], main).astype(jnp.bfloat16)
    vals_t = mm(wvt_ref[...], main).astype(jnp.bfloat16)
    for h in range(A_HEADS):
        at = slice(h * NOPE, (h + 1) * NOPE)
        kx[h, :TOK, :NOPE] = keys[:, at]
        kx[h, TOK:, :NOPE] = k_ref[:, at]
        vx[h, :TOK, :] = vals[:, at]
        vx[h, TOK:, :] = v_ref[:, at]
        ktx[h, :NOPE, :TOK] = keys_t[at, :]
        ktx[h, :NOPE, TOK:] = kt_ref[at, :]
        vtx[h, :, :TOK] = vals_t[at, :]
        vtx[h, :, TOK:] = vt_ref[at, :]

    for h in range(A_HEADS):
        at = slice(h * NOPE, (h + 1) * NOPE)
        q = q_ref[:, h * PAD : (h + 1) * PAD]
        d_out_t = dot_ref[at, :]
        scores = mm(kx[h], q, NT) * (SCALE * LOG2E) + bias[...]
        top = jnp.max(scores, 0, keepdims=True)
        expons = jnp.exp2(scores - top)
        probs = expons * (1.0 / jnp.sum(expons, 0, keepdims=True))
        probs_b = probs.astype(jnp.bfloat16)
        out_t = mm(vtx[h], probs_b).astype(jnp.bfloat16)
        ot_ref[at, :] = out_t
        row_dot = jnp.sum(
            d_out_t.astype(jnp.float32) * out_t.astype(jnp.float32), 0, keepdims=True
        )
        dprob = mm(vx[h], d_out_t)
        dscore = (probs * ((dprob - row_dot) * SCALE)).astype(jnp.bfloat16)
        dqt_ref[h * WIDTH : (h + 1) * WIDTH, :] = mm(ktx[h], dscore).astype(jnp.bfloat16)
        dk = mm(dscore, q).astype(jnp.bfloat16)
        dv = mm(probs_b, d_out_t, NT).astype(jnp.bfloat16)
        dkp[:, at] = dk[:TOK, :NOPE]
        dvp[:, at] = dv[:TOK]
        dk_ref[:, at] = dk[TOK:, :NOPE]
        dv_ref[:, at] = dv[TOK:]
        rope[...] += dk[:, NOPE:].astype(jnp.float32)

    acc[...] += mm(wk_ref[...], dkp[...], NT) + mm(wv_ref[...], dvp[...], NT)

    @pl.when(step == pl.num_programs(0) - 1)
    def _():
        rope_t = rope[...].T
        early_ref[:KVL, :] = acc[...].astype(jnp.bfloat16)
        early_ref[KVL:, :] = rope_t[:ROPE, :TOK].astype(jnp.bfloat16)
        own_rope_ref[...] = rope_t[:ROPE, TOK:]


def attend(lead, kvt, pkvt, q, k, v, kt, vt, d_out_t, wk, wv, wkt, wvt):
    n = HEAD_DEV // A_HEADS
    cols = A_HEADS * NOPE
    whole = lambda *shape: pl.BlockSpec(shape, lambda i: (0,) * len(shape))
    across = lambda rows, width: pl.BlockSpec((rows, width), lambda i: (0, i))
    down = lambda rows, width: pl.BlockSpec((rows, width), lambda i: (i, 0))
    shape = jax.ShapeDtypeStruct
    bf16 = jnp.bfloat16
    return pl.pallas_call(
        attend_kernel,
        grid=(n,),
        in_specs=[
            pl.BlockSpec(memory_space=pltpu.SMEM),
            whole(KVL + ROPE, TOK),
            whole(KVL + ROPE, TOK),
            across(TOK, A_HEADS * PAD),
            across(TOK, cols),
            across(TOK, cols),
            down(cols, TOK),
            down(cols, TOK),
            down(cols, TOK),
            across(KVL, cols),
            across(KVL, cols),
            down(cols, KVL),
            down(cols, KVL),
        ],
        out_specs=[
            down(cols, TOK),
            down(A_HEADS * WIDTH, TOK),
            across(TOK, cols),
            across(TOK, cols),
            whole(KVL + ROPE, TOK),
            whole(ROPE, TOK),
        ],
        out_shape=[
            shape((HEAD_DEV * VDIM, TOK), bf16),
            shape((HEAD_DEV * WIDTH, TOK), bf16),
            shape((TOK, HEAD_DEV * NOPE), bf16),
            shape((TOK, HEAD_DEV * VDIM), bf16),
            shape((KVL + ROPE, TOK), bf16),
            shape((ROPE, TOK), jnp.float32),
        ],
        scratch_shapes=[
            pltpu.VMEM((2 * TOK, TOK), jnp.float32),
            pltpu.VMEM((TOK, KVL), bf16),
            pltpu.VMEM((A_HEADS, 2 * TOK, PAD), bf16),
            pltpu.VMEM((A_HEADS, 2 * TOK, VDIM), bf16),
            pltpu.VMEM((A_HEADS, WIDTH, 2 * TOK), bf16),
            pltpu.VMEM((A_HEADS, VDIM, 2 * TOK), bf16),
            pltpu.VMEM((TOK, cols), bf16),
            pltpu.VMEM((TOK, cols), bf16),
            pltpu.VMEM((KVL, TOK), jnp.float32),
            pltpu.VMEM((2 * TOK, PAD - NOPE), jnp.float32),
        ],
        compiler_params=params(),
        name="attend",
    )(lead, kvt, pkvt, q, k, v, kt, vt, d_out_t, wk, wv, wkt, wvt)


G_STEPS = 4


def gradients_kernel(dqt_ref, dk_ref, dv_ref, wq_ref, wk_ref, wv_ref, gq_ref, gkv_ref):
    gq_ref[...] = mm(wq_ref[...], dqt_ref[...]).astype(jnp.bfloat16)
    gkv_ref[...] = mm(wk_ref[...], dk_ref[...], NT) + mm(wv_ref[...], dv_ref[...], NT)


def gradients(dqt, dk, dv, wq, wk, wv):
    whole = lambda *shape: pl.BlockSpec(shape, lambda i: (0,) * len(shape))
    down = lambda rows, width: pl.BlockSpec((rows // G_STEPS, width), lambda i: (i, 0))
    return pl.pallas_call(
        gradients_kernel,
        grid=(G_STEPS,),
        in_specs=[
            whole(HEAD_DEV * WIDTH, TOK),
            whole(TOK, HEAD_DEV * NOPE),
            whole(TOK, HEAD_DEV * VDIM),
            down(QL, HEAD_DEV * WIDTH),
            down(KVL, HEAD_DEV * NOPE),
            down(KVL, HEAD_DEV * VDIM),
        ],
        out_specs=[down(QL, TOK), down(KVL, TOK)],
        out_shape=[
            jax.ShapeDtypeStruct((QL, TOK), jnp.bfloat16),
            jax.ShapeDtypeStruct((KVL, TOK), jnp.float32),
        ],
        compiler_params=params(),
        name="gradients",
    )(dqt, dk, dv, wq, wk, wv)


def on_device(q_latent, kv_latent, w_query, w_key, w_value, d_out):
    peers = lax.axis_size("head")
    blocks = lax.axis_size("ctx")
    q_cols = q_latent.shape[1]
    own = jnp.concatenate([q_latent.T, kv_latent.T], 0)
    copies = jnp.broadcast_to(own, (peers, *own.shape))
    g = lax.all_to_all(copies, "head", 0, 0, tiled=True)
    kvt = g[:, q_cols:, :].reshape(KVL + ROPE, TOK)
    pkvt = lax.ppermute(kvt, "ctx", [(i, i + 1) for i in range(blocks - 1)])
    wkt, wvt, d_out_t = w_key.T, w_value.T, d_out.T
    q, k, v, kt, vt = project(g, kvt, w_query, w_key, w_value, wkt, wvt)
    lead = (lax.axis_index("ctx") == 0).astype(jnp.int32).reshape(1)
    out_t, dqt, dk, dv, early, own_rope = attend(
        lead, kvt, pkvt, q, k, v, kt, vt, d_out_t, w_key, w_value, wkt, wvt
    )
    later = lax.ppermute(early, "ctx", [(i, i - 1) for i in range(1, blocks)])
    gq, gkv = gradients(dqt, dk, dv, w_query, w_key, w_value)
    own_kv = jnp.concatenate([gkv, own_rope], 0)
    gkv = (own_kv + later.astype(jnp.float32)).astype(jnp.bfloat16)
    terms = jnp.concatenate(
        [gq.reshape(peers, q_cols, TOK), gkv.reshape(peers, -1, TOK)], 1
    )
    terms = lax.all_to_all(terms, "head", 0, 0, tiled=True)
    sums = jnp.sum(terms.astype(jnp.float32), 0)
    return out_t.T, sums[:q_cols].T, sums[q_cols:].T


def solution(mesh):
    return jax.shard_map(
        on_device,
        mesh=mesh,
        in_specs=(
            P("ctx", "head"),
            P("ctx", "head"),
            P(None, "head"),
            P(None, "head"),
            P(None, "head"),
            P("ctx", "head"),
        ),
        out_specs=(P("ctx", "head"), P("ctx", "head"), P("ctx", "head")),
        check_vma=False,
    )
```

```python
import math

import jax
import jax.numpy as jnp
from jax import lax
from jax.experimental import pallas as pl
from jax.experimental.pallas import tpu as pltpu
from jax.sharding import PartitionSpec as P

QL = 1536
KVL = 512
ROPE = 64
NOPE = 128
VDIM = 128
WIDTH = NOPE + ROPE
PAD = 256
HEAD_DEV = 16
TOK = 256
SCALE = WIDTH ** (-0.5)
LOG2E = 1.0 / math.log(2.0)
MIB = 1024 * 1024

NN = (((1,), (0,)), ((), ()))
NT = (((1,), (1,)), ((), ()))


def mm(a, b, dims=NN):
    return lax.dot_general(a, b, dims, preferred_element_type=jnp.float32)


def params(mib):
    return pltpu.CompilerParams(vmem_limit_bytes=mib * MIB)


P_HEADS = 4


def project_kernel(g_ref, kvt_ref, wq_ref, wk_ref, wv_ref, wkt_ref, wvt_ref,
                   q_ref, k_ref, v_ref, kt_ref, vt_ref, qlat, kv):
    @pl.when(pl.program_id(0) == 0)
    def _():
        rows = g_ref[:, : QL // 8, :].reshape(QL, TOK)
        for i in range(QL // 256):
            qlat[:, i * 256 : (i + 1) * 256] = rows[i * 256 : (i + 1) * 256].T
        for i in range(KVL // 256):
            kv[:, i * 256 : (i + 1) * 256] = kvt_ref[i * 256 : (i + 1) * 256, :].T

    queries = mm(qlat[...], wq_ref[...]).astype(jnp.bfloat16)
    zeros = jnp.zeros((TOK, PAD - WIDTH), jnp.bfloat16)
    for h in range(P_HEADS):
        q_ref[:, h * PAD : (h + 1) * PAD] = jnp.concatenate(
            [queries[:, h * WIDTH : (h + 1) * WIDTH], zeros], 1
        )
    k_ref[...] = mm(kv[...], wk_ref[...]).astype(jnp.bfloat16)
    v_ref[...] = mm(kv[...], wv_ref[...]).astype(jnp.bfloat16)
    main = kvt_ref[:KVL, :]
    kt_ref[...] = mm(wkt_ref[...], main).astype(jnp.bfloat16)
    vt_ref[...] = mm(wvt_ref[...], main).astype(jnp.bfloat16)


def project(g, kvt, wq, wk, wv, wkt, wvt):
    n = HEAD_DEV // P_HEADS
    cols = P_HEADS * NOPE
    whole = lambda *shape: pl.BlockSpec(shape, lambda i: (0,) * len(shape))
    shape = jax.ShapeDtypeStruct
    return pl.pallas_call(
        project_kernel,
        grid=(n,),
        in_specs=[
            whole(8, (QL + KVL + ROPE) // 8, TOK),
            whole(KVL + ROPE, TOK),
            pl.BlockSpec((QL, P_HEADS * WIDTH), lambda i: (0, i)),
            pl.BlockSpec((KVL, cols), lambda i: (0, i)),
            pl.BlockSpec((KVL, cols), lambda i: (0, i)),
            pl.BlockSpec((cols, KVL), lambda i: (i, 0)),
            pl.BlockSpec((cols, KVL), lambda i: (i, 0)),
        ],
        out_specs=[
            pl.BlockSpec((TOK, P_HEADS * PAD), lambda i: (0, i)),
            pl.BlockSpec((TOK, cols), lambda i: (0, i)),
            pl.BlockSpec((TOK, cols), lambda i: (0, i)),
            pl.BlockSpec((cols, TOK), lambda i: (i, 0)),
            pl.BlockSpec((cols, TOK), lambda i: (i, 0)),
        ],
        out_shape=[
            shape((TOK, HEAD_DEV * PAD), jnp.bfloat16),
            shape((TOK, HEAD_DEV * NOPE), jnp.bfloat16),
            shape((TOK, HEAD_DEV * VDIM), jnp.bfloat16),
            shape((HEAD_DEV * NOPE, TOK), jnp.bfloat16),
            shape((HEAD_DEV * VDIM, TOK), jnp.bfloat16),
        ],
        scratch_shapes=[
            pltpu.VMEM((TOK, QL), jnp.bfloat16),
            pltpu.VMEM((TOK, KVL), jnp.bfloat16),
        ],
        compiler_params=params(24),
        name="project",
    )(g, kvt, wq, wk, wv, wkt, wvt)


A_HEADS = 2


def attend_kernel(lead_ref, kvt_ref, pkvt_ref, q_ref, k_ref, v_ref, kt_ref, vt_ref,
                  dot_ref, wk_ref, wv_ref, wkt_ref, wvt_ref,
                  ot_ref, dqt_ref, dk_ref, dv_ref, early_ref, own_rope_ref,
                  bias, pkv, kx, vx, ktx, vtx, dkp, dvp, acc, rope):
    step = pl.program_id(0)

    @pl.when(step == 0)
    def _():
        key = lax.broadcasted_iota(jnp.int32, (2 * TOK, TOK), 0)
        query = lax.broadcasted_iota(jnp.int32, (2 * TOK, TOK), 1)
        hidden = jnp.where(key < TOK, jnp.where(lead_ref[0] > 0, key + TOK, key - TOK), key - TOK - query)
        bias[...] = jnp.where(hidden > 0, jnp.float32(-1e30), jnp.float32(0.0))
        for i in range(KVL // 256):
            pkv[:, i * 256 : (i + 1) * 256] = pkvt_ref[i * 256 : (i + 1) * 256, :].T
        ropes_t = jnp.concatenate([pkvt_ref[KVL:, :], kvt_ref[KVL:, :]], 1)
        padded = jnp.concatenate([ropes_t, jnp.zeros_like(ropes_t)], 0)
        ropes = padded.T
        for h in range(A_HEADS):
            kx[h, :, NOPE:] = ropes
            ktx[h, NOPE:, :] = ropes_t
        acc[...] = jnp.zeros_like(acc)
        rope[...] = jnp.zeros_like(rope)

    main = pkvt_ref[:KVL, :]
    keys = mm(pkv[...], wk_ref[...]).astype(jnp.bfloat16)
    vals = mm(pkv[...], wv_ref[...]).astype(jnp.bfloat16)
    keys_t = mm(wkt_ref[...], main).astype(jnp.bfloat16)
    vals_t = mm(wvt_ref[...], main).astype(jnp.bfloat16)
    for h in range(A_HEADS):
        at = slice(h * NOPE, (h + 1) * NOPE)
        kx[h, :TOK, :NOPE] = keys[:, at]
        kx[h, TOK:, :NOPE] = k_ref[:, at]
        vx[h, :TOK, :] = vals[:, at]
        vx[h, TOK:, :] = v_ref[:, at]
        ktx[h, :NOPE, :TOK] = keys_t[at, :]
        ktx[h, :NOPE, TOK:] = kt_ref[at, :]
        vtx[h, :, :TOK] = vals_t[at, :]
        vtx[h, :, TOK:] = vt_ref[at, :]

    for h in range(A_HEADS):
        at = slice(h * NOPE, (h + 1) * NOPE)
        q = q_ref[:, h * PAD : (h + 1) * PAD]
        d_out_t = dot_ref[at, :]
        scores = mm(kx[h], q, NT) * (SCALE * LOG2E) + bias[...]
        top = jnp.max(scores, 0, keepdims=True)
        expons = jnp.exp2(scores - top)
        probs = expons * (1.0 / jnp.sum(expons, 0, keepdims=True))
        probs_b = probs.astype(jnp.bfloat16)
        out_t = mm(vtx[h], probs_b).astype(jnp.bfloat16)
        ot_ref[at, :] = out_t
        row_dot = jnp.sum(
            d_out_t.astype(jnp.float32) * out_t.astype(jnp.float32), 0, keepdims=True
        )
        dprob = mm(vx[h], d_out_t)
        dscore = (probs * ((dprob - row_dot) * SCALE)).astype(jnp.bfloat16)
        dqt_ref[h * WIDTH : (h + 1) * WIDTH, :] = mm(ktx[h], dscore).astype(jnp.bfloat16)
        dk = mm(dscore, q).astype(jnp.bfloat16)
        dv = mm(probs_b, d_out_t, NT).astype(jnp.bfloat16)
        dkp[:, at] = dk[:TOK, :NOPE]
        dvp[:, at] = dv[:TOK]
        dk_ref[:, at] = dk[TOK:, :NOPE]
        dv_ref[:, at] = dv[TOK:]
        rope[...] += dk[:, NOPE:].astype(jnp.float32)

    acc[...] += mm(wk_ref[...], dkp[...], NT) + mm(wv_ref[...], dvp[...], NT)

    @pl.when(step == pl.num_programs(0) - 1)
    def _():
        rope_t = rope[...].T
        early_ref[:KVL, :] = acc[...].astype(jnp.bfloat16)
        early_ref[KVL:, :] = rope_t[:ROPE, :TOK].astype(jnp.bfloat16)
        own_rope_ref[...] = rope_t[:ROPE, TOK:]


def attend(lead, kvt, pkvt, q, k, v, kt, vt, d_out_t, wk, wv, wkt, wvt):
    n = HEAD_DEV // A_HEADS
    cols = A_HEADS * NOPE
    whole = lambda *shape: pl.BlockSpec(shape, lambda i: (0,) * len(shape))
    across = lambda rows, width: pl.BlockSpec((rows, width), lambda i: (0, i))
    down = lambda rows, width: pl.BlockSpec((rows, width), lambda i: (i, 0))
    shape = jax.ShapeDtypeStruct
    bf16 = jnp.bfloat16
    return pl.pallas_call(
        attend_kernel,
        grid=(n,),
        in_specs=[
            pl.BlockSpec(memory_space=pltpu.SMEM),
            whole(KVL + ROPE, TOK),
            whole(KVL + ROPE, TOK),
            across(TOK, A_HEADS * PAD),
            across(TOK, cols),
            across(TOK, cols),
            down(cols, TOK),
            down(cols, TOK),
            down(cols, TOK),
            across(KVL, cols),
            across(KVL, cols),
            down(cols, KVL),
            down(cols, KVL),
        ],
        out_specs=[
            down(cols, TOK),
            down(A_HEADS * WIDTH, TOK),
            across(TOK, cols),
            across(TOK, cols),
            whole(KVL + ROPE, TOK),
            whole(ROPE, TOK),
        ],
        out_shape=[
            shape((HEAD_DEV * VDIM, TOK), bf16),
            shape((HEAD_DEV * WIDTH, TOK), bf16),
            shape((TOK, HEAD_DEV * NOPE), bf16),
            shape((TOK, HEAD_DEV * VDIM), bf16),
            shape((KVL + ROPE, TOK), bf16),
            shape((ROPE, TOK), jnp.float32),
        ],
        scratch_shapes=[
            pltpu.VMEM((2 * TOK, TOK), jnp.float32),
            pltpu.VMEM((TOK, KVL), bf16),
            pltpu.VMEM((A_HEADS, 2 * TOK, PAD), bf16),
            pltpu.VMEM((A_HEADS, 2 * TOK, VDIM), bf16),
            pltpu.VMEM((A_HEADS, WIDTH, 2 * TOK), bf16),
            pltpu.VMEM((A_HEADS, VDIM, 2 * TOK), bf16),
            pltpu.VMEM((TOK, cols), bf16),
            pltpu.VMEM((TOK, cols), bf16),
            pltpu.VMEM((KVL, TOK), jnp.float32),
            pltpu.VMEM((2 * TOK, PAD - NOPE), jnp.float32),
        ],
        compiler_params=params(20),
        name="attend",
    )(lead, kvt, pkvt, q, k, v, kt, vt, d_out_t, wk, wv, wkt, wvt)


G_STEPS = 4


def gradients_kernel(dqt_ref, dk_ref, dv_ref, wq_ref, wk_ref, wv_ref, gq_ref, gkv_ref):
    gq_ref[...] = mm(wq_ref[...], dqt_ref[...]).astype(jnp.bfloat16)
    gkv_ref[...] = mm(wk_ref[...], dk_ref[...], NT) + mm(wv_ref[...], dv_ref[...], NT)


def gradients(dqt, dk, dv, wq, wk, wv):
    whole = lambda *shape: pl.BlockSpec(shape, lambda i: (0,) * len(shape))
    down = lambda rows, width: pl.BlockSpec((rows // G_STEPS, width), lambda i: (i, 0))
    return pl.pallas_call(
        gradients_kernel,
        grid=(G_STEPS,),
        in_specs=[
            whole(HEAD_DEV * WIDTH, TOK),
            whole(TOK, HEAD_DEV * NOPE),
            whole(TOK, HEAD_DEV * VDIM),
            down(QL, HEAD_DEV * WIDTH),
            down(KVL, HEAD_DEV * NOPE),
            down(KVL, HEAD_DEV * VDIM),
        ],
        out_specs=[down(QL, TOK), down(KVL, TOK)],
        out_shape=[
            jax.ShapeDtypeStruct((QL, TOK), jnp.bfloat16),
            jax.ShapeDtypeStruct((KVL, TOK), jnp.float32),
        ],
        compiler_params=params(20),
        name="gradients",
    )(dqt, dk, dv, wq, wk, wv)


def on_device(q_latent, kv_latent, w_query, w_key, w_value, d_out):
    peers = lax.axis_size("head")
    blocks = lax.axis_size("ctx")
    q_cols = q_latent.shape[1]
    own = jnp.concatenate([q_latent.T, kv_latent.T], 0)
    copies = jnp.broadcast_to(own, (peers, *own.shape))
    g = lax.all_to_all(copies, "head", 0, 0, tiled=True)
    wkt, wvt, d_out_t = w_key.T, w_value.T, d_out.T
    g, wkt, wvt, d_out_t = lax.optimization_barrier((g, wkt, wvt, d_out_t))
    kvt = g[:, q_cols:, :].reshape(KVL + ROPE, TOK)
    pkvt = lax.ppermute(kvt, "ctx", [(i, i + 1) for i in range(blocks - 1)])
    q, k, v, kt, vt = project(g, kvt, w_query, w_key, w_value, wkt, wvt)
    lead = (lax.axis_index("ctx") == 0).astype(jnp.int32).reshape(1)
    out_t, dqt, dk, dv, early, own_rope = attend(
        lead, kvt, pkvt, q, k, v, kt, vt, d_out_t, w_key, w_value, wkt, wvt
    )
    later = lax.ppermute(early, "ctx", [(i, i - 1) for i in range(1, blocks)])
    gq, gkv = gradients(dqt, dk, dv, w_query, w_key, w_value)
    own_kv = jnp.concatenate([gkv, own_rope], 0)
    gkv = (own_kv + later.astype(jnp.float32)).astype(jnp.bfloat16)
    terms = jnp.concatenate(
        [gq.reshape(peers, q_cols, TOK), gkv.reshape(peers, -1, TOK)], 1
    )
    terms = lax.all_to_all(terms, "head", 0, 0, tiled=True)
    sums = jnp.sum(terms.astype(jnp.float32), 0)
    return out_t.T, sums[:q_cols].T, sums[q_cols:].T


def solution(mesh):
    return jax.shard_map(
        on_device,
        mesh=mesh,
        in_specs=(
            P("ctx", "head"),
            P("ctx", "head"),
            P(None, "head"),
            P(None, "head"),
            P(None, "head"),
            P("ctx", "head"),
        ),
        out_specs=(P("ctx", "head"), P("ctx", "head"), P("ctx", "head")),
        check_vma=False,
    )
```

```python
import math

import jax
import jax.numpy as jnp
from jax import lax
from jax.experimental import pallas as pl
from jax.experimental.pallas import tpu as pltpu
from jax.sharding import PartitionSpec as P

QL = 1536
KVL = 512
ROPE = 64
NOPE = 128
VDIM = 128
WIDTH = NOPE + ROPE
PAD = 256
HEAD_DEV = 16
TOK = 256
HALF = TOK // 2
PEERS = 8
Q_ROWS = QL // PEERS
KV_ROWS = (KVL + ROPE) // PEERS
SCALE = WIDTH ** (-0.5)
EXPONENT = SCALE / math.log(2.0)
HIDDEN = -1e30
MIB = 1024 * 1024

NN = (((1,), (0,)), ((), ()))
NT = (((1,), (1,)), ((), ()))
BF16 = jnp.bfloat16
F32 = jnp.float32


def mm(a, b, dims=NN):
    return lax.dot_general(a, b, dims, preferred_element_type=F32)


def kernel_call(body, name, out_shape, *args, mib=16, scratch=(), spaces=None):
    vmem = pl.BlockSpec(memory_space=pltpu.VMEM)
    if spaces is None:
        spaces = [pltpu.VMEM] * len(args)
    args = [
        pltpu.with_memory_space_constraint(a, pltpu.VMEM) if s is pltpu.VMEM else a
        for a, s in zip(args, spaces)
    ]
    return pl.pallas_call(
        body,
        in_specs=[pl.BlockSpec(memory_space=s) for s in spaces],
        out_specs=[vmem] * len(out_shape),
        out_shape=[pltpu.VMEM(shape, dtype) for shape, dtype in out_shape],
        scratch_shapes=list(scratch),
        compiler_params=pltpu.CompilerParams(vmem_limit_bytes=mib * MIB),
        name=name,
    )(*args)


def stage_kernel(*refs):
    n = len(refs) // 2
    sems = refs[-1]
    copies = [
        pltpu.make_async_copy(refs[i], refs[n + i], sems.at[i]) for i in range(n)
    ]
    for copy in copies:
        copy.start()
    for copy in copies:
        copy.wait()


def stage(*arrays):
    return kernel_call(
        stage_kernel,
        "stage",
        [(a.shape, a.dtype) for a in arrays],
        *arrays,
        scratch=[pltpu.SemaphoreType.DMA((len(arrays),))],
        spaces=[pl.ANY] * len(arrays),
    )


P_HEADS = 4


def project_kernel(g_ref, wq_ref, wk_ref, wv_ref, q_ref, k_ref, v_ref, kvt_ref):
    for i in range(PEERS):
        kvt_ref[i * KV_ROWS : (i + 1) * KV_ROWS, :] = g_ref[i, Q_ROWS:, :]
    kv = kvt_ref[:KVL, :].T
    k_ref[...] = mm(kv, wk_ref[...]).astype(BF16)
    v_ref[...] = mm(kv, wv_ref[...]).astype(BF16)
    qlat = g_ref[:, :Q_ROWS, :].reshape(QL, TOK).T
    lane = lax.broadcasted_iota(jnp.int32, (TOK, PAD - WIDTH), 1)
    one = jnp.where(lane == 0, 1.0, 0.0).astype(BF16)
    cols = P_HEADS * WIDTH
    for i in range(HEAD_DEV // P_HEADS):
        queries = mm(qlat, wq_ref[:, i * cols : (i + 1) * cols]).astype(BF16)
        for j in range(P_HEADS):
            h = i * P_HEADS + j
            q_ref[:, h * PAD : (h + 1) * PAD] = jnp.concatenate(
                [queries[:, j * WIDTH : (j + 1) * WIDTH], one], 1
            )


def project(g, wq, wk, wv):
    return kernel_call(
        project_kernel,
        "project",
        [
            ((TOK, HEAD_DEV * PAD), BF16),
            ((TOK, HEAD_DEV * NOPE), BF16),
            ((TOK, HEAD_DEV * VDIM), BF16),
            ((KVL + ROPE, TOK), BF16),
        ],
        g, wq, wk, wv,
    )


def attend_kernel(lead_ref, kvt_ref, pkvt_ref, q_ref, k_ref, v_ref, do_ref, wk_ref, wv_ref,
                  out_ref, dqt_ref, dk_ref, dv_ref, early_ref, own_rope_ref,
                  kp, vp, dkp, dvp):
    pkv = pkvt_ref[:KVL, :].T
    kp[...] = mm(pkv, wk_ref[...]).astype(BF16)
    vp[...] = mm(pkv, wv_ref[...]).astype(BF16)
    ropes_t = jnp.concatenate([pkvt_ref[KVL:, :], kvt_ref[KVL:, :]], 1)
    at_row = lax.broadcasted_iota(jnp.int32, (ROPE, 2 * TOK), 0)
    at_key = lax.broadcasted_iota(jnp.int32, (ROPE, 2 * TOK), 1)
    shut = jnp.where(lead_ref[0] > 0, HIDDEN, 0.0)
    marks_t = jnp.where((at_row == 0) & (at_key < TOK), shut, 0.0).astype(BF16)
    ropes = jnp.concatenate([ropes_t, marks_t], 0).T
    key = lax.broadcasted_iota(jnp.int32, (HALF, HALF), 0)
    query = lax.broadcasted_iota(jnp.int32, (HALF, HALF), 1)
    seen = key <= query
    rope_sum = [None]

    def head(h):
        at = slice(h * NOPE, (h + 1) * NOPE)
        q = q_ref[:, h * PAD : (h + 1) * PAD]
        keys = jnp.concatenate([kp[:, at], k_ref[:, at]], 0)
        vals = jnp.concatenate([vp[:, at], v_ref[:, at]], 0)
        d_out_h = do_ref[:, at]
        d_out_t = d_out_h.T
        scores = mm(jnp.concatenate([keys, ropes], 1), q, NT)
        yield
        s_p = scores[:TOK]
        s_a = jnp.concatenate(
            [
                jnp.where(seen, scores[TOK : TOK + HALF, :HALF], HIDDEN),
                scores[TOK : TOK + HALF, HALF:],
            ],
            1,
        )
        s_b = jnp.where(seen, scores[TOK + HALF :, HALF:], HIDDEN)
        top = jnp.maximum(
            jnp.max(s_p, 0, keepdims=True), jnp.max(s_a, 0, keepdims=True)
        )
        top_b = jnp.maximum(top[:, HALF:], jnp.max(s_b, 0, keepdims=True))
        top = jnp.concatenate([top[:, :HALF], top_b], 1)
        yield
        e_p = jnp.exp2((s_p - top) * EXPONENT)
        e_a = jnp.exp2((s_a - top) * EXPONENT)
        e_b = jnp.exp2((s_b - top_b) * EXPONENT)
        total = jnp.sum(e_p, 0, keepdims=True) + jnp.sum(e_a, 0, keepdims=True)
        total = jnp.concatenate(
            [total[:, :HALF], total[:, HALF:] + jnp.sum(e_b, 0, keepdims=True)], 1
        )
        yield
        inv = 1.0 / total
        p_p, p_a, p_b = e_p * inv, e_a * inv, e_b * inv[:, HALF:]
        none = jnp.zeros((HALF, HALF), BF16)
        probs = jnp.concatenate(
            [
                p_p.astype(BF16),
                p_a.astype(BF16),
                jnp.concatenate([none, p_b.astype(BF16)], 1),
            ],
            0,
        )
        yield
        out_t = mm(vals.T, probs).astype(BF16)
        dprob = mm(vals, d_out_t)
        yield
        out_ref[:, at] = out_t.T
        row_dot = jnp.sum(d_out_t.astype(F32) * out_t.astype(F32), 0, keepdims=True)
        yield
        d_p = (p_p * ((dprob[:TOK] - row_dot) * SCALE)).astype(BF16)
        d_a = (p_a * ((dprob[TOK : TOK + HALF] - row_dot) * SCALE)).astype(BF16)
        d_b = (p_b * ((dprob[TOK + HALF :, HALF:] - row_dot[:, HALF:]) * SCALE)).astype(BF16)
        dscore = jnp.concatenate([d_p, d_a, jnp.concatenate([none, d_b], 1)], 0)
        yield
        dqt = mm(jnp.concatenate([keys.T, ropes_t], 0), dscore)
        dk = mm(dscore, q)
        dv = mm(probs, d_out_h)
        yield
        dqt_ref[h * WIDTH : (h + 1) * WIDTH, :] = dqt.astype(BF16)
        dk = dk.astype(BF16)
        dv = dv.astype(BF16)
        dkp[:, at] = dk[:TOK, :NOPE]
        dvp[:, at] = dv[:TOK]
        dk_ref[:, at] = dk[TOK:, :NOPE]
        dv_ref[:, at] = dv[TOK:]
        rope = dk[:, NOPE:].astype(F32)
        rope_sum[0] = rope if rope_sum[0] is None else rope_sum[0] + rope

    skewed(head, HEAD_DEV, LAG)
    early_ref[:KVL, :] = (
        mm(wk_ref[...], dkp[...], NT) + mm(wv_ref[...], dvp[...], NT)
    ).astype(BF16)
    rope_t = rope_sum[0].T
    early_ref[KVL:, :] = rope_t[:ROPE, :TOK].astype(BF16)
    own_rope_ref[...] = rope_t[:ROPE, TOK:]


LAG = 4


def skewed(make, count, lag):
    running = []
    made = 0
    step = 0
    while made < count or running:
        if made < count and step % lag == 0:
            running.append(make(made))
            made += 1
        running = [r for r in running if next(r, True) is None]
        step += 1


def attend(lead, kvt, pkvt, q, k, v, d_out, wk, wv):
    return kernel_call(
        attend_kernel,
        "attend",
        [
            ((TOK, HEAD_DEV * VDIM), BF16),
            ((HEAD_DEV * WIDTH, TOK), BF16),
            ((TOK, HEAD_DEV * NOPE), BF16),
            ((TOK, HEAD_DEV * VDIM), BF16),
            ((KVL + ROPE, TOK), BF16),
            ((ROPE, TOK), F32),
        ],
        lead, kvt, pkvt, q, k, v, d_out, wk, wv,
        scratch=[pltpu.VMEM((TOK, HEAD_DEV * NOPE), BF16)] * 4,
        spaces=[pltpu.SMEM] + [pltpu.VMEM] * 8,
    )


def gradients_kernel(dqt_ref, dk_ref, dv_ref, wq_ref, wk_ref, wv_ref, terms_ref, gkv_ref):
    gkv_ref[...] = mm(wk_ref[...], dk_ref[...], NT) + mm(wv_ref[...], dv_ref[...], NT)
    for i in range(PEERS // 2):
        rows = slice(2 * i * Q_ROWS, 2 * (i + 1) * Q_ROWS)
        part = mm(wq_ref[rows, :], dqt_ref[...]).astype(BF16)
        terms_ref[2 * i, :Q_ROWS, :] = part[:Q_ROWS]
        terms_ref[2 * i + 1, :Q_ROWS, :] = part[Q_ROWS:]


def gradients(dqt, dk, dv, wq, wk, wv):
    return kernel_call(
        gradients_kernel,
        "gradients",
        [((PEERS, Q_ROWS, TOK), BF16), ((KVL, TOK), F32)],
        dqt, dk, dv, wq, wk, wv,
    )


def on_device(q_latent, kv_latent, w_query, w_key, w_value, d_out):
    peers = lax.axis_size("head")
    blocks = lax.axis_size("ctx")
    own = jnp.concatenate([q_latent.T, kv_latent.T], 0)
    copies = jnp.broadcast_to(own, (peers, *own.shape))
    g = lax.all_to_all(copies, "head", 0, 0, tiled=True)
    w_query, w_key, w_value, d_out = stage(w_query, w_key, w_value, d_out)
    g, w_query, w_key, w_value, d_out = lax.optimization_barrier(
        (g, w_query, w_key, w_value, d_out)
    )
    sent = g[:, Q_ROWS:, :].reshape(KVL + ROPE, TOK)
    pkvt = lax.ppermute(sent, "ctx", [(i, i + 1) for i in range(blocks - 1)])
    q, k, v, kvt = project(g, w_query, w_key, w_value)
    lead = (lax.axis_index("ctx") == 0).astype(jnp.int32).reshape(1)
    out, dqt, dk, dv, early, own_rope = attend(
        lead, kvt, pkvt, q, k, v, d_out, w_key, w_value
    )
    later = lax.ppermute(early, "ctx", [(i, i - 1) for i in range(1, blocks)])
    gq, gkv = gradients(dqt, dk, dv, w_query, w_key, w_value)
    own_kv = jnp.concatenate([gkv, own_rope], 0)
    gkv = (own_kv + later.astype(F32)).astype(BF16)
    terms = jnp.concatenate([gq, gkv.reshape(peers, -1, TOK)], 1)
    terms = lax.all_to_all(terms, "head", 0, 0, tiled=True)
    sums = jnp.sum(terms.astype(F32), 0)
    return out, sums[:Q_ROWS].T, sums[Q_ROWS:].T


def solution(mesh):
    return jax.shard_map(
        on_device,
        mesh=mesh,
        in_specs=(
            P("ctx", "head"),
            P("ctx", "head"),
            P(None, "head"),
            P(None, "head"),
            P(None, "head"),
            P("ctx", "head"),
        ),
        out_specs=(P("ctx", "head"), P("ctx", "head"), P("ctx", "head")),
        check_vma=False,
    )
```

```python
import math

import jax
import jax.numpy as jnp
from jax import lax
from jax.experimental import pallas as pl
from jax.experimental.pallas import tpu as pltpu
from jax.sharding import PartitionSpec as P

QL = 1536
KVL = 512
ROPE = 64
NOPE = 128
VDIM = 128
WIDTH = NOPE + ROPE
PAD = 256
HEAD_DEV = 16
TOK = 256
HALF = TOK // 2
PEERS = 8
Q_ROWS = QL // PEERS
KV_ROWS = (KVL + ROPE) // PEERS
SCALE = WIDTH ** (-0.5)
EXPONENT = SCALE / math.log(2.0)
HIDDEN = -1e30
MIB = 1024 * 1024

NN = (((1,), (0,)), ((), ()))
NT = (((1,), (1,)), ((), ()))
BF16 = jnp.bfloat16
F32 = jnp.float32


def mm(a, b, dims=NN):
    return lax.dot_general(a, b, dims, preferred_element_type=F32)


def kernel_call(body, name, out_shape, *args, mib=16, scratch=(), spaces=None):
    vmem = pl.BlockSpec(memory_space=pltpu.VMEM)
    if spaces is None:
        spaces = [pltpu.VMEM] * len(args)
    args = [
        pltpu.with_memory_space_constraint(a, s) if s in (pltpu.VMEM, pltpu.HBM) else a
        for a, s in zip(args, spaces)
    ]
    return pl.pallas_call(
        body,
        in_specs=[pl.BlockSpec(memory_space=s or pltpu.VMEM) for s in spaces],
        out_specs=[vmem] * len(out_shape),
        out_shape=[pltpu.VMEM(shape, dtype) for shape, dtype in out_shape],
        scratch_shapes=list(scratch),
        compiler_params=pltpu.CompilerParams(vmem_limit_bytes=mib * MIB),
        name=name,
    )(*args)


P_HEADS = 4
P_STEPS = HEAD_DEV // P_HEADS


def project_kernel(g_ref, wq_hbm, wk_hbm, wv_hbm, do_hbm,
                   q_ref, k_ref, v_ref, kvt_ref, wk_ref, wv_ref, do_ref, wq_ref, sems):
    cols = P_HEADS * WIDTH
    part = lambda i: slice(i * cols, (i + 1) * cols)
    wq_in = [
        pltpu.make_async_copy(wq_hbm.at[:, part(i)], wq_ref.at[:, part(i)], sems.at[i])
        for i in range(P_STEPS)
    ]
    wk_in = pltpu.make_async_copy(wk_hbm, wk_ref, sems.at[P_STEPS])
    wv_in = pltpu.make_async_copy(wv_hbm, wv_ref, sems.at[P_STEPS + 1])
    do_in = pltpu.make_async_copy(do_hbm, do_ref, sems.at[P_STEPS + 2])
    order = [wk_in, *wq_in[:1], wv_in, *wq_in[1:], do_in]
    for copy in order:
        copy.start()
    for i in range(PEERS):
        kvt_ref[i * KV_ROWS : (i + 1) * KV_ROWS, :] = g_ref[i, Q_ROWS:, :]
    kv = kvt_ref[:KVL, :].T
    qlat = g_ref[:, :Q_ROWS, :].reshape(QL, TOK).T
    lane = lax.broadcasted_iota(jnp.int32, (TOK, PAD - WIDTH), 1)
    one = jnp.where(lane == 0, 1.0, 0.0).astype(BF16)

    def project_queries(i):
        wq_in[i].wait()
        queries = mm(qlat, wq_ref[:, part(i)]).astype(BF16)
        for j in range(P_HEADS):
            h = i * P_HEADS + j
            q_ref[:, h * PAD : (h + 1) * PAD] = jnp.concatenate(
                [queries[:, j * WIDTH : (j + 1) * WIDTH], one], 1
            )

    wk_in.wait()
    k_ref[...] = mm(kv, wk_ref[...]).astype(BF16)
    project_queries(0)
    wv_in.wait()
    v_ref[...] = mm(kv, wv_ref[...]).astype(BF16)
    for i in range(1, P_STEPS):
        project_queries(i)
    do_in.wait()


def project(g, wq, wk, wv, d_out):
    return kernel_call(
        project_kernel,
        "project",
        [
            ((TOK, HEAD_DEV * PAD), BF16),
            ((TOK, HEAD_DEV * NOPE), BF16),
            ((TOK, HEAD_DEV * VDIM), BF16),
            ((KVL + ROPE, TOK), BF16),
            (wk.shape, BF16),
            (wv.shape, BF16),
            (d_out.shape, BF16),
        ],
        g, wq, wk, wv, d_out,
        mib=20,
        scratch=[pltpu.VMEM(wq.shape, BF16), pltpu.SemaphoreType.DMA((P_STEPS + 3,))],
        spaces=[None] + [pltpu.HBM] * 4,
    )


def attend_kernel(lead_ref, kvt_ref, pkvt_ref, q_ref, k_ref, v_ref, do_ref, wk_ref, wv_ref,
                  out_ref, dqt_ref, dk_ref, dv_ref, early_ref, own_rope_ref,
                  kp, vp, dkp, dvp):
    pkv = pkvt_ref[:KVL, :].T
    kp[...] = mm(pkv, wk_ref[...]).astype(BF16)
    vp[...] = mm(pkv, wv_ref[...]).astype(BF16)
    ropes_t = jnp.concatenate([pkvt_ref[KVL:, :], kvt_ref[KVL:, :]], 1)
    at_row = lax.broadcasted_iota(jnp.int32, (ROPE, 2 * TOK), 0)
    at_key = lax.broadcasted_iota(jnp.int32, (ROPE, 2 * TOK), 1)
    shut = jnp.where(lead_ref[0] > 0, HIDDEN, 0.0)
    marks_t = jnp.where((at_row == 0) & (at_key < TOK), shut, 0.0).astype(BF16)
    ropes = jnp.concatenate([ropes_t, marks_t], 0).T
    key = lax.broadcasted_iota(jnp.int32, (HALF, HALF), 0)
    query = lax.broadcasted_iota(jnp.int32, (HALF, HALF), 1)
    seen = key <= query
    rope_sum = [None]

    def head(h):
        at = slice(h * NOPE, (h + 1) * NOPE)
        q = q_ref[:, h * PAD : (h + 1) * PAD]
        keys = jnp.concatenate([kp[:, at], k_ref[:, at]], 0)
        vals = jnp.concatenate([vp[:, at], v_ref[:, at]], 0)
        d_out_h = do_ref[:, at]
        d_out_t = d_out_h.T
        scores = mm(jnp.concatenate([keys, ropes], 1), q, NT)
        yield
        s_p = scores[:TOK]
        s_a = jnp.concatenate(
            [
                jnp.where(seen, scores[TOK : TOK + HALF, :HALF], HIDDEN),
                scores[TOK : TOK + HALF, HALF:],
            ],
            1,
        )
        s_b = jnp.where(seen, scores[TOK + HALF :, HALF:], HIDDEN)
        top = jnp.maximum(
            jnp.max(s_p, 0, keepdims=True), jnp.max(s_a, 0, keepdims=True)
        )
        top_b = jnp.maximum(top[:, HALF:], jnp.max(s_b, 0, keepdims=True))
        top = jnp.concatenate([top[:, :HALF], top_b], 1)
        yield
        e_p = jnp.exp2((s_p - top) * EXPONENT)
        e_a = jnp.exp2((s_a - top) * EXPONENT)
        e_b = jnp.exp2((s_b - top_b) * EXPONENT)
        total = jnp.sum(e_p, 0, keepdims=True) + jnp.sum(e_a, 0, keepdims=True)
        total = jnp.concatenate(
            [total[:, :HALF], total[:, HALF:] + jnp.sum(e_b, 0, keepdims=True)], 1
        )
        yield
        inv = 1.0 / total
        p_p, p_a, p_b = e_p * inv, e_a * inv, e_b * inv[:, HALF:]
        none = jnp.zeros((HALF, HALF), BF16)
        probs = jnp.concatenate(
            [
                p_p.astype(BF16),
                p_a.astype(BF16),
                jnp.concatenate([none, p_b.astype(BF16)], 1),
            ],
            0,
        )
        yield
        out_t = mm(vals.T, probs).astype(BF16)
        dprob = mm(vals, d_out_t)
        yield
        out_ref[:, at] = out_t.T
        row_dot = jnp.sum(d_out_t.astype(F32) * out_t.astype(F32), 0, keepdims=True)
        yield
        d_p = (p_p * ((dprob[:TOK] - row_dot) * SCALE)).astype(BF16)
        d_a = (p_a * ((dprob[TOK : TOK + HALF] - row_dot) * SCALE)).astype(BF16)
        d_b = (p_b * ((dprob[TOK + HALF :, HALF:] - row_dot[:, HALF:]) * SCALE)).astype(BF16)
        dscore = jnp.concatenate([d_p, d_a, jnp.concatenate([none, d_b], 1)], 0)
        yield
        dqt = mm(jnp.concatenate([keys.T, ropes_t], 0), dscore)
        dk = mm(dscore, q)
        dv = mm(probs, d_out_h)
        yield
        dqt_ref[h * WIDTH : (h + 1) * WIDTH, :] = dqt.astype(BF16)
        dk = dk.astype(BF16)
        dv = dv.astype(BF16)
        dkp[:, at] = dk[:TOK, :NOPE]
        dvp[:, at] = dv[:TOK]
        dk_ref[:, at] = dk[TOK:, :NOPE]
        dv_ref[:, at] = dv[TOK:]
        rope = dk[:, NOPE:].astype(F32)
        rope_sum[0] = rope if rope_sum[0] is None else rope_sum[0] + rope

    skewed(head, HEAD_DEV, LAG)
    early_ref[:KVL, :] = (
        mm(wk_ref[...], dkp[...], NT) + mm(wv_ref[...], dvp[...], NT)
    ).astype(BF16)
    rope_t = rope_sum[0].T
    early_ref[KVL:, :] = rope_t[:ROPE, :TOK].astype(BF16)
    own_rope_ref[...] = rope_t[:ROPE, TOK:]


LAG = 4


def skewed(make, count, lag):
    running = []
    made = 0
    step = 0
    while made < count or running:
        if made < count and step % lag == 0:
            running.append(make(made))
            made += 1
        running = [r for r in running if next(r, True) is None]
        step += 1


def attend(lead, kvt, pkvt, q, k, v, d_out, wk, wv):
    return kernel_call(
        attend_kernel,
        "attend",
        [
            ((TOK, HEAD_DEV * VDIM), BF16),
            ((HEAD_DEV * WIDTH, TOK), BF16),
            ((TOK, HEAD_DEV * NOPE), BF16),
            ((TOK, HEAD_DEV * VDIM), BF16),
            ((KVL + ROPE, TOK), BF16),
            ((ROPE, TOK), F32),
        ],
        lead, kvt, pkvt, q, k, v, d_out, wk, wv,
        scratch=[pltpu.VMEM((TOK, HEAD_DEV * NOPE), BF16)] * 4,
        spaces=[pltpu.SMEM] + [pltpu.VMEM] * 8,
    )


G_STEPS = PEERS // 2


def gradients_kernel(dqt_ref, dk_ref, dv_ref, wq_hbm, wk_ref, wv_ref,
                     terms_ref, gkv_ref, wq_ref, sems):
    part = lambda i: slice(2 * i * Q_ROWS, 2 * (i + 1) * Q_ROWS)
    wq_in = [
        pltpu.make_async_copy(wq_hbm.at[part(i), :], wq_ref.at[part(i), :], sems.at[i])
        for i in range(G_STEPS)
    ]
    for copy in wq_in:
        copy.start()
    gkv_ref[...] = mm(wk_ref[...], dk_ref[...], NT) + mm(wv_ref[...], dv_ref[...], NT)
    for i in range(G_STEPS):
        wq_in[i].wait()
        rows = mm(wq_ref[part(i), :], dqt_ref[...]).astype(BF16)
        terms_ref[2 * i, :Q_ROWS, :] = rows[:Q_ROWS]
        terms_ref[2 * i + 1, :Q_ROWS, :] = rows[Q_ROWS:]


def gradients(dqt, dk, dv, wq, wk, wv):
    return kernel_call(
        gradients_kernel,
        "gradients",
        [((PEERS, Q_ROWS, TOK), BF16), ((KVL, TOK), F32)],
        dqt, dk, dv, wq, wk, wv,
        mib=16,
        scratch=[pltpu.VMEM(wq.shape, BF16), pltpu.SemaphoreType.DMA((G_STEPS,))],
        spaces=[pltpu.VMEM] * 3 + [pltpu.HBM] + [pltpu.VMEM] * 2,
    )


def pack_kernel(q_ref, kv_ref, out_ref):
    for i in range(PEERS):
        out_ref[i, :Q_ROWS, :] = q_ref[...]
        out_ref[i, Q_ROWS:, :] = kv_ref[...]


def pack(q_t, kv_t):
    return pl.pallas_call(
        pack_kernel,
        out_shape=jax.ShapeDtypeStruct((PEERS, Q_ROWS + KV_ROWS, TOK), BF16),
        name="pack",
    )(q_t, kv_t)


def total_kernel(terms_ref, q_ref, kv_ref):
    sums = jnp.sum(terms_ref[...].astype(F32), 0)
    q_ref[...] = sums[:Q_ROWS]
    kv_ref[...] = sums[Q_ROWS:]


def total(terms):
    return pl.pallas_call(
        total_kernel,
        out_shape=[
            jax.ShapeDtypeStruct((Q_ROWS, TOK), F32),
            jax.ShapeDtypeStruct((KV_ROWS, TOK), F32),
        ],
        in_specs=[pl.BlockSpec(memory_space=pltpu.VMEM)],
        name="total",
    )(pltpu.with_memory_space_constraint(terms, pltpu.VMEM))


def on_device(q_latent, kv_latent, w_query, w_key, w_value, d_out):
    peers = lax.axis_size("head")
    blocks = lax.axis_size("ctx")
    copies = pack(q_latent.T, kv_latent.T)
    g = lax.all_to_all(copies, "head", 0, 0, tiled=True)
    sent = g[:, Q_ROWS:, :].reshape(KVL + ROPE, TOK)
    pkvt = lax.ppermute(sent, "ctx", [(i, i + 1) for i in range(blocks - 1)])
    q, k, v, kvt, wk_in, wv_in, do_in = project(g, w_query, w_key, w_value, d_out)
    lead = (lax.axis_index("ctx") == 0).astype(jnp.int32).reshape(1)
    out, dqt, dk, dv, early, own_rope = attend(
        lead, kvt, pkvt, q, k, v, do_in, wk_in, wv_in
    )
    later = lax.ppermute(early, "ctx", [(i, i - 1) for i in range(1, blocks)])
    gq, gkv = gradients(dqt, dk, dv, w_query, wk_in, wv_in)
    own_kv = jnp.concatenate([gkv, own_rope], 0)
    gkv = (own_kv + later.astype(F32)).astype(BF16)
    terms = jnp.concatenate([gq, gkv.reshape(peers, -1, TOK)], 1)
    terms = lax.all_to_all(terms, "head", 0, 0, tiled=True)
    gq, gkv = total(terms)
    return out, gq.T, gkv.T


def solution(mesh):
    return jax.shard_map(
        on_device,
        mesh=mesh,
        in_specs=(
            P("ctx", "head"),
            P("ctx", "head"),
            P(None, "head"),
            P(None, "head"),
            P(None, "head"),
            P("ctx", "head"),
        ),
        out_specs=(P("ctx", "head"), P("ctx", "head"), P("ctx", "head")),
        check_vma=False,
    )
```

```python
import math

import jax
import jax.numpy as jnp
from jax import lax
from jax.experimental import pallas as pl
from jax.experimental.pallas import tpu as pltpu
from jax.sharding import PartitionSpec as P

QL = 1536
KVL = 512
ROPE = 64
NOPE = 128
VDIM = 128
WIDTH = NOPE + ROPE
PAD = 256
HEAD_DEV = 16
TOK = 256
HALF = TOK // 2
PEERS = 8
Q_ROWS = QL // PEERS
KV_ROWS = (KVL + ROPE) // PEERS
SCALE = WIDTH ** (-0.5)
EXPONENT = SCALE / math.log(2.0)
HIDDEN = -1e30
MIB = 1024 * 1024

NN = (((1,), (0,)), ((), ()))
NT = (((1,), (1,)), ((), ()))
BF16 = jnp.bfloat16
F32 = jnp.float32


def mm(a, b, dims=NN):
    return lax.dot_general(a, b, dims, preferred_element_type=F32)


def kernel_call(body, name, out_shape, *args, mib=16, scratch=(), spaces=None, hbm_outs=0):
    outs = [pltpu.HBM] * hbm_outs + [pltpu.VMEM] * (len(out_shape) - hbm_outs)
    if spaces is None:
        spaces = [pltpu.VMEM] * len(args)
    args = [
        pltpu.with_memory_space_constraint(a, s) if s in (pltpu.VMEM, pltpu.HBM) else a
        for a, s in zip(args, spaces)
    ]
    return pl.pallas_call(
        body,
        in_specs=[pl.BlockSpec(memory_space=s or pltpu.VMEM) for s in spaces],
        out_specs=[pl.BlockSpec(memory_space=s) for s in outs],
        out_shape=[s(shape, dtype) for s, (shape, dtype) in zip(outs, out_shape)],
        scratch_shapes=list(scratch),
        compiler_params=pltpu.CompilerParams(vmem_limit_bytes=mib * MIB),
        name=name,
    )(*args)


P_HEADS = 4
P_STEPS = HEAD_DEV // P_HEADS


def project_kernel(g_ref, wq_hbm, wk_hbm, wv_hbm, do_hbm,
                   q_ref, k_ref, v_ref, kvt_ref, wk_ref, wv_ref, do_ref, wq_ref, sems):
    cols = P_HEADS * WIDTH
    part = lambda i: slice(i * cols, (i + 1) * cols)
    wq_in = [
        pltpu.make_async_copy(wq_hbm.at[:, part(i)], wq_ref.at[:, part(i)], sems.at[i])
        for i in range(P_STEPS)
    ]
    wk_in = pltpu.make_async_copy(wk_hbm, wk_ref, sems.at[P_STEPS])
    wv_in = pltpu.make_async_copy(wv_hbm, wv_ref, sems.at[P_STEPS + 1])
    do_in = pltpu.make_async_copy(do_hbm, do_ref, sems.at[P_STEPS + 2])
    order = [wk_in, wq_in[0], wv_in, *wq_in[1:], do_in]
    order[0].start()
    order[1].start()

    def arrived(i):
        order[i].wait()
        if i + 2 < len(order):
            order[i + 2].start()

    for i in range(PEERS):
        kvt_ref[i * KV_ROWS : (i + 1) * KV_ROWS, :] = g_ref[i, Q_ROWS:, :]
    kv = kvt_ref[:KVL, :].T
    qlat = g_ref[:, :Q_ROWS, :].reshape(QL, TOK).T
    lane = lax.broadcasted_iota(jnp.int32, (TOK, PAD - WIDTH), 1)
    one = jnp.where(lane == 0, 1.0, 0.0).astype(BF16)

    def project_queries(i):
        queries = mm(qlat, wq_ref[:, part(i)]).astype(BF16)
        for j in range(P_HEADS):
            h = i * P_HEADS + j
            q_ref[:, h * PAD : (h + 1) * PAD] = jnp.concatenate(
                [queries[:, j * WIDTH : (j + 1) * WIDTH], one], 1
            )

    arrived(0)
    k_ref[...] = mm(kv, wk_ref[...]).astype(BF16)
    arrived(1)
    project_queries(0)
    arrived(2)
    v_ref[...] = mm(kv, wv_ref[...]).astype(BF16)
    for i in range(1, P_STEPS):
        arrived(2 + i)
        project_queries(i)
    arrived(2 + P_STEPS)


def project(g, wq, wk, wv, d_out):
    return kernel_call(
        project_kernel,
        "project",
        [
            ((TOK, HEAD_DEV * PAD), BF16),
            ((TOK, HEAD_DEV * NOPE), BF16),
            ((TOK, HEAD_DEV * VDIM), BF16),
            ((KVL + ROPE, TOK), BF16),
            (wk.shape, BF16),
            (wv.shape, BF16),
            (d_out.shape, BF16),
        ],
        g, wq, wk, wv, d_out,
        mib=20,
        scratch=[pltpu.VMEM(wq.shape, BF16), pltpu.SemaphoreType.DMA((P_STEPS + 3,))],
        spaces=[None] + [pltpu.HBM] * 4,
    )


def attend_kernel(lead_ref, kvt_ref, pkvt_ref, q_ref, k_ref, v_ref, do_ref, wk_ref, wv_ref, wq_hbm,
                  out_hbm, dqt_ref, dk_ref, dv_ref, early_ref, own_rope_ref, wq_ref,
                  kp, vp, dkp, dvp, out_ref, sems):
    wq_in = pltpu.make_async_copy(wq_hbm, wq_ref, sems.at[O_STEPS])
    wq_in.start()
    wide = HEAD_DEV * VDIM // O_STEPS
    out_copies = [
        pltpu.make_async_copy(
            out_ref.at[:, i * wide : (i + 1) * wide],
            out_hbm.at[:, i * wide : (i + 1) * wide],
            sems.at[i],
        )
        for i in range(O_STEPS)
    ]
    pkv = pkvt_ref[:KVL, :].T
    kp[...] = mm(pkv, wk_ref[...]).astype(BF16)
    vp[...] = mm(pkv, wv_ref[...]).astype(BF16)
    ropes_t = jnp.concatenate([pkvt_ref[KVL:, :], kvt_ref[KVL:, :]], 1)
    at_row = lax.broadcasted_iota(jnp.int32, (ROPE, 2 * TOK), 0)
    at_key = lax.broadcasted_iota(jnp.int32, (ROPE, 2 * TOK), 1)
    shut = jnp.where(lead_ref[0] > 0, HIDDEN, 0.0)
    marks_t = jnp.where((at_row == 0) & (at_key < TOK), shut, 0.0).astype(BF16)
    ropes = jnp.concatenate([ropes_t, marks_t], 0).T
    key = lax.broadcasted_iota(jnp.int32, (HALF, HALF), 0)
    query = lax.broadcasted_iota(jnp.int32, (HALF, HALF), 1)
    seen = key <= query
    rope_sum = [None]

    def head(h):
        at = slice(h * NOPE, (h + 1) * NOPE)
        q = q_ref[:, h * PAD : (h + 1) * PAD]
        keys = jnp.concatenate([kp[:, at], k_ref[:, at]], 0)
        vals = jnp.concatenate([vp[:, at], v_ref[:, at]], 0)
        d_out_h = do_ref[:, at]
        d_out_t = d_out_h.T
        scores = mm(jnp.concatenate([keys, ropes], 1), q, NT)
        yield
        s_p = scores[:TOK]
        s_a = jnp.concatenate(
            [
                jnp.where(seen, scores[TOK : TOK + HALF, :HALF], HIDDEN),
                scores[TOK : TOK + HALF, HALF:],
            ],
            1,
        )
        s_b = jnp.where(seen, scores[TOK + HALF :, HALF:], HIDDEN)
        top = jnp.maximum(
            jnp.max(s_p, 0, keepdims=True), jnp.max(s_a, 0, keepdims=True)
        )
        top_b = jnp.maximum(top[:, HALF:], jnp.max(s_b, 0, keepdims=True))
        top = jnp.concatenate([top[:, :HALF], top_b], 1)
        yield
        e_p = jnp.exp2((s_p - top) * EXPONENT)
        e_a = jnp.exp2((s_a - top) * EXPONENT)
        e_b = jnp.exp2((s_b - top_b) * EXPONENT)
        total = jnp.sum(e_p, 0, keepdims=True) + jnp.sum(e_a, 0, keepdims=True)
        total = jnp.concatenate(
            [total[:, :HALF], total[:, HALF:] + jnp.sum(e_b, 0, keepdims=True)], 1
        )
        yield
        inv = 1.0 / total
        p_p, p_a, p_b = e_p * inv, e_a * inv, e_b * inv[:, HALF:]
        none = jnp.zeros((HALF, HALF), BF16)
        probs = jnp.concatenate(
            [
                p_p.astype(BF16),
                p_a.astype(BF16),
                jnp.concatenate([none, p_b.astype(BF16)], 1),
            ],
            0,
        )
        yield
        out_t = mm(vals.T, probs).astype(BF16)
        dprob = mm(vals, d_out_t)
        yield
        out_ref[:, at] = out_t.T
        row_dot = jnp.sum(d_out_t.astype(F32) * out_t.astype(F32), 0, keepdims=True)
        yield
        d_p = (p_p * ((dprob[:TOK] - row_dot) * SCALE)).astype(BF16)
        d_a = (p_a * ((dprob[TOK : TOK + HALF] - row_dot) * SCALE)).astype(BF16)
        d_b = (p_b * ((dprob[TOK + HALF :, HALF:] - row_dot[:, HALF:]) * SCALE)).astype(BF16)
        dscore = jnp.concatenate([d_p, d_a, jnp.concatenate([none, d_b], 1)], 0)
        yield
        dqt = mm(jnp.concatenate([keys.T, ropes_t], 0), dscore)
        dk = mm(dscore, q)
        dv = mm(probs, d_out_h)
        yield
        dqt_ref[h * WIDTH : (h + 1) * WIDTH, :] = dqt.astype(BF16)
        dk = dk.astype(BF16)
        dv = dv.astype(BF16)
        dkp[:, at] = dk[:TOK, :NOPE]
        dvp[:, at] = dv[:TOK]
        dk_ref[:, at] = dk[TOK:, :NOPE]
        dv_ref[:, at] = dv[TOK:]
        rope = dk[:, NOPE:].astype(F32)
        rope_sum[0] = rope if rope_sum[0] is None else rope_sum[0] + rope
        if (h + 1) % (HEAD_DEV // O_STEPS) == 0:
            out_copies[h // (HEAD_DEV // O_STEPS)].start()

    skewed(head, HEAD_DEV, LAG)
    early_ref[:KVL, :] = (
        mm(wk_ref[...], dkp[...], NT) + mm(wv_ref[...], dvp[...], NT)
    ).astype(BF16)
    rope_t = rope_sum[0].T
    early_ref[KVL:, :] = rope_t[:ROPE, :TOK].astype(BF16)
    own_rope_ref[...] = rope_t[:ROPE, TOK:]
    for copy in out_copies:
        copy.wait()
    wq_in.wait()


LAG = 4
O_STEPS = 4


def skewed(make, count, lag):
    running = []
    made = 0
    step = 0
    while made < count or running:
        if made < count and step % lag == 0:
            running.append(make(made))
            made += 1
        running = [r for r in running if next(r, True) is None]
        step += 1


def attend(lead, kvt, pkvt, q, k, v, d_out, wk, wv, wq):
    return kernel_call(
        attend_kernel,
        "attend",
        [
            ((TOK, HEAD_DEV * VDIM), BF16),
            ((HEAD_DEV * WIDTH, TOK), BF16),
            ((TOK, HEAD_DEV * NOPE), BF16),
            ((TOK, HEAD_DEV * VDIM), BF16),
            ((KVL + ROPE, TOK), BF16),
            ((ROPE, TOK), F32),
            (wq.shape, BF16),
        ],
        lead, kvt, pkvt, q, k, v, d_out, wk, wv, wq,
        mib=20,
        scratch=[pltpu.VMEM((TOK, HEAD_DEV * NOPE), BF16)] * 5
        + [pltpu.SemaphoreType.DMA((O_STEPS + 1,))],
        spaces=[pltpu.SMEM] + [pltpu.VMEM] * 8 + [pltpu.HBM],
        hbm_outs=1,
    )


G_STEPS = PEERS // 2


def gradients_kernel(dqt_ref, dk_ref, dv_ref, wq_ref, wk_ref, wv_ref, terms_ref, gkv_ref):
    gkv_ref[...] = mm(wk_ref[...], dk_ref[...], NT) + mm(wv_ref[...], dv_ref[...], NT)
    for i in range(G_STEPS):
        part = slice(2 * i * Q_ROWS, 2 * (i + 1) * Q_ROWS)
        rows = mm(wq_ref[part, :], dqt_ref[...]).astype(BF16)
        terms_ref[2 * i, :Q_ROWS, :] = rows[:Q_ROWS]
        terms_ref[2 * i + 1, :Q_ROWS, :] = rows[Q_ROWS:]


def gradients(dqt, dk, dv, wq, wk, wv):
    return kernel_call(
        gradients_kernel,
        "gradients",
        [((PEERS, Q_ROWS, TOK), BF16), ((KVL, TOK), F32)],
        dqt, dk, dv, wq, wk, wv,
        mib=8,
    )


def total_kernel(terms_ref, q_ref, kv_ref):
    sums = jnp.sum(terms_ref[...].astype(F32), 0)
    q_ref[...] = sums[:Q_ROWS]
    kv_ref[...] = sums[Q_ROWS:]


def total(terms):
    return pl.pallas_call(
        total_kernel,
        out_shape=[
            jax.ShapeDtypeStruct((Q_ROWS, TOK), F32),
            jax.ShapeDtypeStruct((KV_ROWS, TOK), F32),
        ],
        in_specs=[pl.BlockSpec(memory_space=pltpu.VMEM)],
        name="total",
    )(pltpu.with_memory_space_constraint(terms, pltpu.VMEM))


def on_device(q_latent, kv_latent, w_query, w_key, w_value, d_out):
    peers = lax.axis_size("head")
    blocks = lax.axis_size("ctx")
    own = jnp.concatenate([q_latent.T, kv_latent.T], 0)
    copies = jnp.broadcast_to(own, (peers, *own.shape))
    g = lax.all_to_all(copies, "head", 0, 0, tiled=True)
    sent = g[:, Q_ROWS:, :].reshape(KVL + ROPE, TOK)
    pkvt = lax.ppermute(sent, "ctx", [(i, i + 1) for i in range(blocks - 1)])
    q, k, v, kvt, wk_in, wv_in, do_in = project(g, w_query, w_key, w_value, d_out)
    lead = (lax.axis_index("ctx") == 0).astype(jnp.int32).reshape(1)
    out, dqt, dk, dv, early, own_rope, wq_in = attend(
        lead, kvt, pkvt, q, k, v, do_in, wk_in, wv_in, w_query
    )
    later = lax.ppermute(early, "ctx", [(i, i - 1) for i in range(1, blocks)])
    gq, gkv = gradients(dqt, dk, dv, wq_in, wk_in, wv_in)
    own_kv = jnp.concatenate([gkv, own_rope], 0)
    gkv = (own_kv + later.astype(F32)).astype(BF16)
    terms = jnp.concatenate([gq, gkv.reshape(peers, -1, TOK)], 1)
    terms = lax.all_to_all(terms, "head", 0, 0, tiled=True)
    gq, gkv = total(terms)
    return out, gq.T, gkv.T


def solution(mesh):
    return jax.shard_map(
        on_device,
        mesh=mesh,
        in_specs=(
            P("ctx", "head"),
            P("ctx", "head"),
            P(None, "head"),
            P(None, "head"),
            P(None, "head"),
            P("ctx", "head"),
        ),
        out_specs=(P("ctx", "head"), P("ctx", "head"), P("ctx", "head")),
        check_vma=False,
    )
```

```python
import math

import jax
import jax.numpy as jnp
from jax import lax
from jax.experimental import pallas as pl
from jax.experimental.pallas import tpu as pltpu
from jax.sharding import PartitionSpec as P

QL = 1536
KVL = 512
ROPE = 64
NOPE = 128
VDIM = 128
WIDTH = NOPE + ROPE
PAD = 256
HEAD_DEV = 16
TOK = 256
HALF = TOK // 2
PEERS = 8
Q_ROWS = QL // PEERS
KV_ROWS = (KVL + ROPE) // PEERS
SCALE = WIDTH ** (-0.5)
EXPONENT = SCALE / math.log(2.0)
HIDDEN = -1e30
MIB = 1024 * 1024

NN = (((1,), (0,)), ((), ()))
NT = (((1,), (1,)), ((), ()))
BF16 = jnp.bfloat16
F32 = jnp.float32


def mm(a, b, dims=NN):
    return lax.dot_general(a, b, dims, preferred_element_type=F32)


def kernel_call(body, name, out_shape, *args, mib=16, scratch=(), spaces=None, hbm_outs=0):
    outs = [pltpu.HBM] * hbm_outs + [pltpu.VMEM] * (len(out_shape) - hbm_outs)
    if spaces is None:
        spaces = [pltpu.VMEM] * len(args)
    args = [
        pltpu.with_memory_space_constraint(a, s) if s in (pltpu.VMEM, pltpu.HBM) else a
        for a, s in zip(args, spaces)
    ]
    return pl.pallas_call(
        body,
        in_specs=[pl.BlockSpec(memory_space=s or pltpu.VMEM) for s in spaces],
        out_specs=[pl.BlockSpec(memory_space=s) for s in outs],
        out_shape=[s(shape, dtype) for s, (shape, dtype) in zip(outs, out_shape)],
        scratch_shapes=list(scratch),
        compiler_params=pltpu.CompilerParams(vmem_limit_bytes=mib * MIB),
        name=name,
    )(*args)


P_HEADS = 4
P_STEPS = HEAD_DEV // P_HEADS


def project_kernel(g_ref, wq_hbm, wk_hbm, wv_hbm, do_hbm,
                   q_ref, k_ref, v_ref, kvt_ref, wk_ref, wv_ref, do_ref, wq_ref, sems):
    cols = P_HEADS * WIDTH
    part = lambda i: slice(i * cols, (i + 1) * cols)
    wq_in = [
        pltpu.make_async_copy(wq_hbm.at[:, part(i)], wq_ref.at[:, part(i)], sems.at[i])
        for i in range(P_STEPS)
    ]
    wk_in = pltpu.make_async_copy(wk_hbm, wk_ref, sems.at[P_STEPS])
    wv_in = pltpu.make_async_copy(wv_hbm, wv_ref, sems.at[P_STEPS + 1])
    do_in = pltpu.make_async_copy(do_hbm, do_ref, sems.at[P_STEPS + 2])
    order = [wk_in, wq_in[0], wv_in, *wq_in[1:], do_in]
    order[0].start()
    order[1].start()

    def arrived(i):
        order[i].wait()
        if i + 2 < len(order):
            order[i + 2].start()

    for i in range(PEERS):
        kvt_ref[i * KV_ROWS : (i + 1) * KV_ROWS, :] = g_ref[i, Q_ROWS:, :]
    kv = kvt_ref[:KVL, :].T
    qlat = g_ref[:, :Q_ROWS, :].reshape(QL, TOK).T
    lane = lax.broadcasted_iota(jnp.int32, (TOK, PAD - WIDTH), 1)
    one = jnp.where(lane == 0, 1.0, 0.0).astype(BF16)

    def project_queries(i):
        queries = mm(qlat, wq_ref[:, part(i)]).astype(BF16)
        for j in range(P_HEADS):
            h = i * P_HEADS + j
            q_ref[:, h * PAD : (h + 1) * PAD] = jnp.concatenate(
                [queries[:, j * WIDTH : (j + 1) * WIDTH], one], 1
            )

    arrived(0)
    k_ref[...] = mm(kv, wk_ref[...]).astype(BF16)
    arrived(1)
    project_queries(0)
    arrived(2)
    v_ref[...] = mm(kv, wv_ref[...]).astype(BF16)
    for i in range(1, P_STEPS):
        arrived(2 + i)
        project_queries(i)
    arrived(2 + P_STEPS)


def project(g, wq, wk, wv, d_out):
    return kernel_call(
        project_kernel,
        "project",
        [
            ((TOK, HEAD_DEV * PAD), BF16),
            ((TOK, HEAD_DEV * NOPE), BF16),
            ((TOK, HEAD_DEV * VDIM), BF16),
            ((KVL + ROPE, TOK), BF16),
            (wk.shape, BF16),
            (wv.shape, BF16),
            (d_out.shape, BF16),
        ],
        g, wq, wk, wv, d_out,
        mib=20,
        scratch=[pltpu.VMEM(wq.shape, BF16), pltpu.SemaphoreType.DMA((P_STEPS + 3,))],
        spaces=[None] + [pltpu.HBM] * 4,
    )


def attend_kernel(lead_ref, kvt_ref, pkvt_ref, q_ref, k_ref, v_ref, do_ref, wk_ref, wv_ref, wq_hbm,
                  out_hbm, ds_ref, po_ref, kp, early_ref, wq_ref,
                  vp, dkp, dvp, out_ref, sems):
    wq_in = pltpu.make_async_copy(wq_hbm, wq_ref, sems.at[O_STEPS])
    wq_in.start()
    wide = HEAD_DEV * VDIM // O_STEPS
    out_copies = [
        pltpu.make_async_copy(
            out_ref.at[:, i * wide : (i + 1) * wide],
            out_hbm.at[:, i * wide : (i + 1) * wide],
            sems.at[i],
        )
        for i in range(O_STEPS)
    ]
    pkv = pkvt_ref[:KVL, :].T
    kp[...] = mm(pkv, wk_ref[...]).astype(BF16)
    vp[...] = mm(pkv, wv_ref[...]).astype(BF16)
    ropes_t = jnp.concatenate([pkvt_ref[KVL:, :], kvt_ref[KVL:, :]], 1)
    at_row = lax.broadcasted_iota(jnp.int32, (ROPE, 2 * TOK), 0)
    at_key = lax.broadcasted_iota(jnp.int32, (ROPE, 2 * TOK), 1)
    shut = jnp.where(lead_ref[0] > 0, HIDDEN, 0.0)
    marks_t = jnp.where((at_row == 0) & (at_key < TOK), shut, 0.0).astype(BF16)
    ropes = jnp.concatenate([ropes_t, marks_t], 0).T
    key = lax.broadcasted_iota(jnp.int32, (HALF, HALF), 0)
    query = lax.broadcasted_iota(jnp.int32, (HALF, HALF), 1)
    seen = key <= query
    rope_sum = [None]

    def head(h):
        at = slice(h * NOPE, (h + 1) * NOPE)
        q = q_ref[:, h * PAD : (h + 1) * PAD]
        keys = jnp.concatenate([kp[:, at], k_ref[:, at]], 0)
        vals = jnp.concatenate([vp[:, at], v_ref[:, at]], 0)
        d_out_h = do_ref[:, at]
        d_out_t = d_out_h.T
        scores = mm(jnp.concatenate([keys, ropes], 1), q, NT)
        yield
        s_p = scores[:TOK]
        s_a = jnp.concatenate(
            [
                jnp.where(seen, scores[TOK : TOK + HALF, :HALF], HIDDEN),
                scores[TOK : TOK + HALF, HALF:],
            ],
            1,
        )
        s_b = jnp.where(seen, scores[TOK + HALF :, HALF:], HIDDEN)
        top = jnp.maximum(
            jnp.max(s_p, 0, keepdims=True), jnp.max(s_a, 0, keepdims=True)
        )
        top_b = jnp.maximum(top[:, HALF:], jnp.max(s_b, 0, keepdims=True))
        top = jnp.concatenate([top[:, :HALF], top_b], 1)
        yield
        e_p = jnp.exp2((s_p - top) * EXPONENT)
        e_a = jnp.exp2((s_a - top) * EXPONENT)
        e_b = jnp.exp2((s_b - top_b) * EXPONENT)
        total = jnp.sum(e_p, 0, keepdims=True) + jnp.sum(e_a, 0, keepdims=True)
        total = jnp.concatenate(
            [total[:, :HALF], total[:, HALF:] + jnp.sum(e_b, 0, keepdims=True)], 1
        )
        yield
        inv = 1.0 / total
        p_p, p_a, p_b = e_p * inv, e_a * inv, e_b * inv[:, HALF:]
        none = jnp.zeros((HALF, HALF), BF16)
        probs = jnp.concatenate(
            [
                p_p.astype(BF16),
                p_a.astype(BF16),
                jnp.concatenate([none, p_b.astype(BF16)], 1),
            ],
            0,
        )
        yield
        out_t = mm(vals.T, probs).astype(BF16)
        dprob = mm(vals, d_out_t)
        yield
        out_ref[:, at] = out_t.T
        row_dot = jnp.sum(d_out_t.astype(F32) * out_t.astype(F32), 0, keepdims=True)
        yield
        d_p = (p_p * ((dprob[:TOK] - row_dot) * SCALE)).astype(BF16)
        d_a = (p_a * ((dprob[TOK : TOK + HALF] - row_dot) * SCALE)).astype(BF16)
        d_b = (p_b * ((dprob[TOK + HALF :, HALF:] - row_dot[:, HALF:]) * SCALE)).astype(BF16)
        dscore = jnp.concatenate([d_p, d_a, jnp.concatenate([none, d_b], 1)], 0)
        yield
        ds_ref[h] = dscore
        po_ref[h] = probs[TOK:]
        dk = mm(dscore[:TOK], q)
        dv = mm(probs[:TOK], d_out_h)
        yield
        dk = dk.astype(BF16)
        dkp[:, at] = dk[:, :NOPE]
        dvp[:, at] = dv.astype(BF16)
        rope = dk[:, NOPE:].astype(F32)
        rope_sum[0] = rope if rope_sum[0] is None else rope_sum[0] + rope
        if (h + 1) % (HEAD_DEV // O_STEPS) == 0:
            out_copies[h // (HEAD_DEV // O_STEPS)].start()

    skewed(head, HEAD_DEV, LAG)
    early_ref[:KVL, :] = (
        mm(wk_ref[...], dkp[...], NT) + mm(wv_ref[...], dvp[...], NT)
    ).astype(BF16)
    early_ref[KVL:, :] = rope_sum[0].T[:ROPE].astype(BF16)
    for copy in out_copies:
        copy.wait()
    wq_in.wait()


LAG = 4
O_STEPS = 4


def skewed(make, count, lag):
    running = []
    made = 0
    step = 0
    while made < count or running:
        if made < count and step % lag == 0:
            running.append(make(made))
            made += 1
        running = [r for r in running if next(r, True) is None]
        step += 1


def attend(lead, kvt, pkvt, q, k, v, d_out, wk, wv, wq):
    return kernel_call(
        attend_kernel,
        "attend",
        [
            ((TOK, HEAD_DEV * VDIM), BF16),
            ((HEAD_DEV, 2 * TOK, TOK), BF16),
            ((HEAD_DEV, TOK, TOK), BF16),
            ((TOK, HEAD_DEV * NOPE), BF16),
            ((KVL + ROPE, TOK), BF16),
            (wq.shape, BF16),
        ],
        lead, kvt, pkvt, q, k, v, d_out, wk, wv, wq,
        mib=20,
        scratch=[pltpu.VMEM((TOK, HEAD_DEV * NOPE), BF16)] * 4
        + [pltpu.SemaphoreType.DMA((O_STEPS + 1,))],
        spaces=[pltpu.SMEM] + [pltpu.VMEM] * 8 + [pltpu.HBM],
        hbm_outs=1,
    )


G_STEPS = PEERS // 2


def gradients_kernel(ds_ref, po_ref, kp_ref, k_ref, kvt_ref, pkvt_ref, q_ref, do_ref,
                     wq_ref, wk_ref, wv_ref, terms_ref, gkv_ref, dqt, dko, dvo):
    ropes_t = jnp.concatenate([pkvt_ref[KVL:, :], kvt_ref[KVL:, :]], 1)
    rope_sum = None
    for h in range(HEAD_DEV):
        at = slice(h * NOPE, (h + 1) * NOPE)
        keys_t = jnp.concatenate([kp_ref[:, at], k_ref[:, at]], 0).T
        dqt[h * WIDTH : (h + 1) * WIDTH, :] = mm(
            jnp.concatenate([keys_t, ropes_t], 0), ds_ref[h]
        ).astype(BF16)
        dk = mm(ds_ref[h, TOK:, :], q_ref[:, h * PAD : (h + 1) * PAD]).astype(BF16)
        dko[:, at] = dk[:, :NOPE]
        dvo[:, at] = mm(po_ref[h], do_ref[:, at]).astype(BF16)
        rope = dk[:, NOPE:].astype(F32)
        rope_sum = rope if rope_sum is None else rope_sum + rope
    gkv_ref[:KVL, :] = mm(wk_ref[...], dko[...], NT) + mm(wv_ref[...], dvo[...], NT)
    gkv_ref[KVL:, :] = rope_sum.T[:ROPE]
    for i in range(G_STEPS):
        part = slice(2 * i * Q_ROWS, 2 * (i + 1) * Q_ROWS)
        rows = mm(wq_ref[part, :], dqt[...]).astype(BF16)
        terms_ref[2 * i, :Q_ROWS, :] = rows[:Q_ROWS]
        terms_ref[2 * i + 1, :Q_ROWS, :] = rows[Q_ROWS:]


def gradients(ds, po, kp, k, kvt, pkvt, q, d_out, wq, wk, wv):
    return kernel_call(
        gradients_kernel,
        "gradients",
        [((PEERS, Q_ROWS, TOK), BF16), ((KVL + ROPE, TOK), F32)],
        ds, po, kp, k, kvt, pkvt, q, d_out, wq, wk, wv,
        scratch=[
            pltpu.VMEM((HEAD_DEV * WIDTH, TOK), BF16),
            pltpu.VMEM((TOK, HEAD_DEV * NOPE), BF16),
            pltpu.VMEM((TOK, HEAD_DEV * VDIM), BF16),
        ],
    )


def total_kernel(terms_ref, q_ref, kv_ref):
    sums = jnp.sum(terms_ref[...].astype(F32), 0)
    q_ref[...] = sums[:Q_ROWS]
    kv_ref[...] = sums[Q_ROWS:]


def total(terms):
    return pl.pallas_call(
        total_kernel,
        out_shape=[
            jax.ShapeDtypeStruct((Q_ROWS, TOK), F32),
            jax.ShapeDtypeStruct((KV_ROWS, TOK), F32),
        ],
        in_specs=[pl.BlockSpec(memory_space=pltpu.VMEM)],
        name="total",
    )(pltpu.with_memory_space_constraint(terms, pltpu.VMEM))


def on_device(q_latent, kv_latent, w_query, w_key, w_value, d_out):
    peers = lax.axis_size("head")
    blocks = lax.axis_size("ctx")
    own = jnp.concatenate([q_latent.T, kv_latent.T], 0)
    copies = jnp.broadcast_to(own, (peers, *own.shape))
    g = lax.all_to_all(copies, "head", 0, 0, tiled=True)
    sent = g[:, Q_ROWS:, :].reshape(KVL + ROPE, TOK)
    pkvt = lax.ppermute(sent, "ctx", [(i, i + 1) for i in range(blocks - 1)])
    q, k, v, kvt, wk_in, wv_in, do_in = project(g, w_query, w_key, w_value, d_out)
    lead = (lax.axis_index("ctx") == 0).astype(jnp.int32).reshape(1)
    out, ds, po, kp, early, wq_in = attend(
        lead, kvt, pkvt, q, k, v, do_in, wk_in, wv_in, w_query
    )
    later = lax.ppermute(early, "ctx", [(i, i - 1) for i in range(1, blocks)])
    gq, gkv = gradients(
        ds, po, kp, k, kvt, pkvt, q, do_in, wq_in, wk_in, wv_in
    )
    gkv = (gkv + later.astype(F32)).astype(BF16)
    terms = jnp.concatenate([gq, gkv.reshape(peers, -1, TOK)], 1)
    terms = lax.all_to_all(terms, "head", 0, 0, tiled=True)
    gq, gkv = total(terms)
    return out, gq.T, gkv.T


def solution(mesh):
    return jax.shard_map(
        on_device,
        mesh=mesh,
        in_specs=(
            P("ctx", "head"),
            P("ctx", "head"),
            P(None, "head"),
            P(None, "head"),
            P(None, "head"),
            P("ctx", "head"),
        ),
        out_specs=(P("ctx", "head"), P("ctx", "head"), P("ctx", "head")),
        check_vma=False,
    )
```

```python
import math

import jax
import jax.numpy as jnp
from jax import lax
from jax.experimental import pallas as pl
from jax.experimental.pallas import tpu as pltpu
from jax.sharding import PartitionSpec as P

QL = 1536
KVL = 512
ROPE = 64
NOPE = 128
VDIM = 128
WIDTH = NOPE + ROPE
PAD = 256
HEAD_DEV = 16
TOK = 256
HALF = TOK // 2
PEERS = 8
Q_ROWS = QL // PEERS
KV_ROWS = (KVL + ROPE) // PEERS
SCALE = WIDTH ** (-0.5)
EXPONENT = SCALE / math.log(2.0)
HIDDEN = -1e30
MIB = 1024 * 1024

NN = (((1,), (0,)), ((), ()))
NT = (((1,), (1,)), ((), ()))
BF16 = jnp.bfloat16
F32 = jnp.float32


def mm(a, b, dims=NN):
    return lax.dot_general(a, b, dims, preferred_element_type=F32)


def kernel_call(body, name, out_shape, *args, mib=16, scratch=(), spaces=None, hbm_outs=0):
    outs = [pltpu.HBM] * hbm_outs + [pltpu.VMEM] * (len(out_shape) - hbm_outs)
    if spaces is None:
        spaces = [pltpu.VMEM] * len(args)
    args = [
        pltpu.with_memory_space_constraint(a, s) if s in (pltpu.VMEM, pltpu.HBM) else a
        for a, s in zip(args, spaces)
    ]
    return pl.pallas_call(
        body,
        in_specs=[pl.BlockSpec(memory_space=s or pltpu.VMEM) for s in spaces],
        out_specs=[pl.BlockSpec(memory_space=s) for s in outs],
        out_shape=[s(shape, dtype) for s, (shape, dtype) in zip(outs, out_shape)],
        scratch_shapes=list(scratch),
        compiler_params=pltpu.CompilerParams(vmem_limit_bytes=mib * MIB),
        name=name,
    )(*args)


P_HEADS = 4
P_STEPS = HEAD_DEV // P_HEADS


def project_kernel(g_ref, wq_hbm, wk_ref, wv_hbm,
                   q_ref, k_ref, v_ref, kvt_ref, wv_ref, wq_ref, sems):
    cols = P_HEADS * WIDTH
    part = lambda i: slice(i * cols, (i + 1) * cols)
    wq_in = [
        pltpu.make_async_copy(wq_hbm.at[:, part(i)], wq_ref.at[:, part(i)], sems.at[i])
        for i in range(P_STEPS)
    ]
    wv_in = pltpu.make_async_copy(wv_hbm, wv_ref, sems.at[P_STEPS])
    order = [wq_in[0], wv_in, *wq_in[1:]]
    order[0].start()
    order[1].start()

    def arrived(i):
        order[i].wait()
        if i + 2 < len(order):
            order[i + 2].start()

    for i in range(PEERS):
        kvt_ref[i * KV_ROWS : (i + 1) * KV_ROWS, :] = g_ref[i, Q_ROWS:, :]
    kv = kvt_ref[:KVL, :].T
    qlat = g_ref[:, :Q_ROWS, :].reshape(QL, TOK).T
    lane = lax.broadcasted_iota(jnp.int32, (TOK, PAD - WIDTH), 1)
    one = jnp.where(lane == 0, 1.0, 0.0).astype(BF16)

    def project_queries(i):
        queries = mm(qlat, wq_ref[:, part(i)]).astype(BF16)
        for j in range(P_HEADS):
            h = i * P_HEADS + j
            q_ref[:, h * PAD : (h + 1) * PAD] = jnp.concatenate(
                [queries[:, j * WIDTH : (j + 1) * WIDTH], one], 1
            )

    k_ref[...] = mm(kv, wk_ref[...]).astype(BF16)
    arrived(0)
    project_queries(0)
    arrived(1)
    v_ref[...] = mm(kv, wv_ref[...]).astype(BF16)
    for i in range(1, P_STEPS):
        arrived(1 + i)
        project_queries(i)


def project(g, wq, wk, wv):
    return kernel_call(
        project_kernel,
        "project",
        [
            ((TOK, HEAD_DEV * PAD), BF16),
            ((TOK, HEAD_DEV * NOPE), BF16),
            ((TOK, HEAD_DEV * VDIM), BF16),
            ((KVL + ROPE, TOK), BF16),
            (wv.shape, BF16),
        ],
        g, wq, wk, wv,
        mib=20,
        scratch=[pltpu.VMEM(wq.shape, BF16), pltpu.SemaphoreType.DMA((P_STEPS + 1,))],
        spaces=[None, pltpu.HBM, pltpu.VMEM, pltpu.HBM],
    )


def attend_kernel(lead_ref, kvt_ref, pkvt_ref, q_ref, k_ref, v_ref, do_ref, wk_ref, wv_ref, wq_hbm,
                  out_hbm, ds_ref, po_ref, kp, early_ref, wq_ref,
                  vp, dkp, dvp, out_ref, sems):
    wq_in = pltpu.make_async_copy(wq_hbm, wq_ref, sems.at[O_STEPS])
    wq_in.start()
    wide = HEAD_DEV * VDIM // O_STEPS
    out_copies = [
        pltpu.make_async_copy(
            out_ref.at[:, i * wide : (i + 1) * wide],
            out_hbm.at[:, i * wide : (i + 1) * wide],
            sems.at[i],
        )
        for i in range(O_STEPS)
    ]
    pkv = pkvt_ref[:KVL, :].T
    kp[...] = mm(pkv, wk_ref[...]).astype(BF16)
    vp[...] = mm(pkv, wv_ref[...]).astype(BF16)
    ropes_t = jnp.concatenate([pkvt_ref[KVL:, :], kvt_ref[KVL:, :]], 1)
    at_row = lax.broadcasted_iota(jnp.int32, (ROPE, 2 * TOK), 0)
    at_key = lax.broadcasted_iota(jnp.int32, (ROPE, 2 * TOK), 1)
    shut = jnp.where(lead_ref[0] > 0, HIDDEN, 0.0)
    marks_t = jnp.where((at_row == 0) & (at_key < TOK), shut, 0.0).astype(BF16)
    ropes = jnp.concatenate([ropes_t, marks_t], 0).T
    key = lax.broadcasted_iota(jnp.int32, (HALF, HALF), 0)
    query = lax.broadcasted_iota(jnp.int32, (HALF, HALF), 1)
    seen = key <= query
    rope_sum = [None]

    def head(h):
        at = slice(h * NOPE, (h + 1) * NOPE)
        q = q_ref[:, h * PAD : (h + 1) * PAD]
        keys = jnp.concatenate([kp[:, at], k_ref[:, at]], 0)
        vals = jnp.concatenate([vp[:, at], v_ref[:, at]], 0)
        d_out_h = do_ref[:, at]
        d_out_t = d_out_h.T
        scores = mm(jnp.concatenate([keys, ropes], 1), q, NT)
        yield
        s_p = scores[:TOK]
        s_a = jnp.concatenate(
            [
                jnp.where(seen, scores[TOK : TOK + HALF, :HALF], HIDDEN),
                scores[TOK : TOK + HALF, HALF:],
            ],
            1,
        )
        s_b = jnp.where(seen, scores[TOK + HALF :, HALF:], HIDDEN)
        top = jnp.maximum(
            jnp.max(s_p, 0, keepdims=True), jnp.max(s_a, 0, keepdims=True)
        )
        top_b = jnp.maximum(top[:, HALF:], jnp.max(s_b, 0, keepdims=True))
        top = jnp.concatenate([top[:, :HALF], top_b], 1)
        yield
        e_p = jnp.exp2((s_p - top) * EXPONENT)
        e_a = jnp.exp2((s_a - top) * EXPONENT)
        e_b = jnp.exp2((s_b - top_b) * EXPONENT)
        total = jnp.sum(e_p, 0, keepdims=True) + jnp.sum(e_a, 0, keepdims=True)
        total = jnp.concatenate(
            [total[:, :HALF], total[:, HALF:] + jnp.sum(e_b, 0, keepdims=True)], 1
        )
        yield
        inv = 1.0 / total
        invs = inv * SCALE
        none = jnp.zeros((HALF, HALF), BF16)
        probs = jnp.concatenate(
            [
                (e_p * inv).astype(BF16),
                (e_a * inv).astype(BF16),
                jnp.concatenate([none, (e_b * inv[:, HALF:]).astype(BF16)], 1),
            ],
            0,
        )
        yield
        out_t = mm(vals.T, probs).astype(BF16)
        yield
        out_ref[:, at] = out_t.T
        row_dot = jnp.sum(d_out_t.astype(F32) * out_t.astype(F32), 0, keepdims=True)
        yield
        dprob = mm(vals, d_out_t)
        d_p = (e_p * invs * (dprob[:TOK] - row_dot)).astype(BF16)
        d_a = (e_a * invs * (dprob[TOK : TOK + HALF] - row_dot)).astype(BF16)
        d_b = (e_b * invs[:, HALF:] * (dprob[TOK + HALF :, HALF:] - row_dot[:, HALF:])).astype(BF16)
        dscore = jnp.concatenate([d_p, d_a, jnp.concatenate([none, d_b], 1)], 0)
        yield
        ds_ref[h] = dscore
        po_ref[h] = probs[TOK:]
        dk = mm(dscore[:TOK], q)
        dv = mm(probs[:TOK], d_out_h)
        yield
        dk = dk.astype(BF16)
        dkp[:, at] = dk[:, :NOPE]
        dvp[:, at] = dv.astype(BF16)
        rope = dk[:, NOPE:].astype(F32)
        rope_sum[0] = rope if rope_sum[0] is None else rope_sum[0] + rope
        if (h + 1) % (HEAD_DEV // O_STEPS) == 0:
            out_copies[h // (HEAD_DEV // O_STEPS)].start()

    skewed(head, HEAD_DEV, LAG)
    early_ref[:KVL, :] = (
        mm(wk_ref[...], dkp[...], NT) + mm(wv_ref[...], dvp[...], NT)
    ).astype(BF16)
    early_ref[KVL:, :] = rope_sum[0].T[:ROPE].astype(BF16)
    for copy in out_copies:
        copy.wait()
    wq_in.wait()


LAG = 1
O_STEPS = 4


def skewed(make, count, lag):
    running = []
    made = 0
    step = 0
    while made < count or running:
        if made < count and step % lag == 0:
            running.append(make(made))
            made += 1
        running = [r for r in running[::-1] if next(r, True) is None][::-1]
        step += 1


def attend(lead, kvt, pkvt, q, k, v, d_out, wk, wv, wq):
    return kernel_call(
        attend_kernel,
        "attend",
        [
            ((TOK, HEAD_DEV * VDIM), BF16),
            ((HEAD_DEV, 2 * TOK, TOK), BF16),
            ((HEAD_DEV, TOK, TOK), BF16),
            ((TOK, HEAD_DEV * NOPE), BF16),
            ((KVL + ROPE, TOK), BF16),
            (wq.shape, BF16),
        ],
        lead, kvt, pkvt, q, k, v, d_out, wk, wv, wq,
        mib=20,
        scratch=[pltpu.VMEM((TOK, HEAD_DEV * NOPE), BF16)] * 4
        + [pltpu.SemaphoreType.DMA((O_STEPS + 1,))],
        spaces=[pltpu.SMEM] + [pltpu.VMEM] * 8 + [pltpu.HBM],
        hbm_outs=1,
    )


G_STEPS = PEERS // 2


def gradients_kernel(ds_ref, po_ref, kp_ref, k_ref, kvt_ref, pkvt_ref, q_ref, do_ref,
                     wq_ref, wk_ref, wv_ref, terms_ref, gkv_ref, dqt, dko, dvo):
    ropes_t = jnp.concatenate([pkvt_ref[KVL:, :], kvt_ref[KVL:, :]], 1)
    rope_sum = None
    for h in range(HEAD_DEV):
        at = slice(h * NOPE, (h + 1) * NOPE)
        keys_t = jnp.concatenate([kp_ref[:, at], k_ref[:, at]], 0).T
        dqt[h * WIDTH : (h + 1) * WIDTH, :] = mm(
            jnp.concatenate([keys_t, ropes_t], 0), ds_ref[h]
        ).astype(BF16)
        dk = mm(ds_ref[h, TOK:, :], q_ref[:, h * PAD : (h + 1) * PAD]).astype(BF16)
        dko[:, at] = dk[:, :NOPE]
        dvo[:, at] = mm(po_ref[h], do_ref[:, at]).astype(BF16)
        rope = dk[:, NOPE:].astype(F32)
        rope_sum = rope if rope_sum is None else rope_sum + rope
    gkv_ref[:KVL, :] = mm(wk_ref[...], dko[...], NT) + mm(wv_ref[...], dvo[...], NT)
    gkv_ref[KVL:, :] = rope_sum.T[:ROPE]
    for i in range(G_STEPS):
        part = slice(2 * i * Q_ROWS, 2 * (i + 1) * Q_ROWS)
        rows = mm(wq_ref[part, :], dqt[...]).astype(BF16)
        terms_ref[2 * i, :Q_ROWS, :] = rows[:Q_ROWS]
        terms_ref[2 * i + 1, :Q_ROWS, :] = rows[Q_ROWS:]


def gradients(ds, po, kp, k, kvt, pkvt, q, d_out, wq, wk, wv):
    return kernel_call(
        gradients_kernel,
        "gradients",
        [((PEERS, Q_ROWS, TOK), BF16), ((KVL + ROPE, TOK), F32)],
        ds, po, kp, k, kvt, pkvt, q, d_out, wq, wk, wv,
        scratch=[
            pltpu.VMEM((HEAD_DEV * WIDTH, TOK), BF16),
            pltpu.VMEM((TOK, HEAD_DEV * NOPE), BF16),
            pltpu.VMEM((TOK, HEAD_DEV * VDIM), BF16),
        ],
    )


def total_kernel(terms_ref, q_ref, kv_ref):
    sums = jnp.sum(terms_ref[...].astype(F32), 0)
    q_ref[...] = sums[:Q_ROWS]
    kv_ref[...] = sums[Q_ROWS:]


def total(terms):
    return pl.pallas_call(
        total_kernel,
        out_shape=[
            jax.ShapeDtypeStruct((Q_ROWS, TOK), F32),
            jax.ShapeDtypeStruct((KV_ROWS, TOK), F32),
        ],
        in_specs=[pl.BlockSpec(memory_space=pltpu.VMEM)],
        name="total",
    )(pltpu.with_memory_space_constraint(terms, pltpu.VMEM))


def on_device(q_latent, kv_latent, w_query, w_key, w_value, d_out):
    peers = lax.axis_size("head")
    blocks = lax.axis_size("ctx")
    own = jnp.concatenate([q_latent.T, kv_latent.T], 0)
    copies = jnp.broadcast_to(own, (peers, *own.shape))
    g = lax.all_to_all(copies, "head", 0, 0, tiled=True)
    sent = g[:, Q_ROWS:, :].reshape(KVL + ROPE, TOK)
    pkvt = lax.ppermute(sent, "ctx", [(i, i + 1) for i in range(blocks - 1)])
    q, k, v, kvt, wv_in = project(g, w_query, w_key, w_value)
    lead = (lax.axis_index("ctx") == 0).astype(jnp.int32).reshape(1)
    out, ds, po, kp, early, wq_in = attend(
        lead, kvt, pkvt, q, k, v, d_out, w_key, wv_in, w_query
    )
    later = lax.ppermute(early, "ctx", [(i, i - 1) for i in range(1, blocks)])
    gq, gkv = gradients(
        ds, po, kp, k, kvt, pkvt, q, d_out, wq_in, w_key, wv_in
    )
    gkv = (gkv + later.astype(F32)).astype(BF16)
    terms = jnp.concatenate([gq, gkv.reshape(peers, -1, TOK)], 1)
    terms = lax.all_to_all(terms, "head", 0, 0, tiled=True)
    gq, gkv = total(terms)
    return out, gq.T, gkv.T


def solution(mesh):
    return jax.shard_map(
        on_device,
        mesh=mesh,
        in_specs=(
            P("ctx", "head"),
            P("ctx", "head"),
            P(None, "head"),
            P(None, "head"),
            P(None, "head"),
            P("ctx", "head"),
        ),
        out_specs=(P("ctx", "head"), P("ctx", "head"), P("ctx", "head")),
        check_vma=False,
    )
```

```python
import math

import jax
import jax.numpy as jnp
from jax import lax
from jax.experimental import pallas as pl
from jax.experimental.pallas import tpu as pltpu
from jax.sharding import PartitionSpec as P

QL = 1536
KVL = 512
ROPE = 64
NOPE = 128
VDIM = 128
WIDTH = NOPE + ROPE
PAD = 256
HEAD_DEV = 16
TOK = 256
HALF = TOK // 2
PEERS = 8
Q_ROWS = QL // PEERS
KV_ROWS = (KVL + ROPE) // PEERS
SCALE = WIDTH ** (-0.5)
EXPONENT = SCALE / math.log(2.0)
HIDDEN = -1e30
MIB = 1024 * 1024

NN = (((1,), (0,)), ((), ()))
NT = (((1,), (1,)), ((), ()))
BF16 = jnp.bfloat16
F32 = jnp.float32


def mm(a, b, dims=NN):
    return lax.dot_general(a, b, dims, preferred_element_type=F32)


def kernel_call(body, name, out_shape, *args, mib=16, scratch=(), spaces=None, hbm_outs=0):
    outs = [pltpu.HBM] * hbm_outs + [pltpu.VMEM] * (len(out_shape) - hbm_outs)
    if spaces is None:
        spaces = [pltpu.VMEM] * len(args)
    args = [
        pltpu.with_memory_space_constraint(a, s) if s in (pltpu.VMEM, pltpu.HBM) else a
        for a, s in zip(args, spaces)
    ]
    return pl.pallas_call(
        body,
        in_specs=[pl.BlockSpec(memory_space=s or pltpu.VMEM) for s in spaces],
        out_specs=[pl.BlockSpec(memory_space=s) for s in outs],
        out_shape=[s(shape, dtype) for s, (shape, dtype) in zip(outs, out_shape)],
        scratch_shapes=list(scratch),
        compiler_params=pltpu.CompilerParams(vmem_limit_bytes=mib * MIB),
        name=name,
    )(*args)


P_HEADS = 4
P_STEPS = HEAD_DEV // P_HEADS


def project_kernel(g_ref, wq_hbm, wk_ref, wv_hbm,
                   q_ref, k_ref, v_ref, kvt_ref, wv_ref, wq_ref, sems):
    cols = P_HEADS * WIDTH
    part = lambda i: slice(i * cols, (i + 1) * cols)
    wq_in = [
        pltpu.make_async_copy(wq_hbm.at[:, part(i)], wq_ref.at[:, part(i)], sems.at[i])
        for i in range(P_STEPS)
    ]
    wv_in = pltpu.make_async_copy(wv_hbm, wv_ref, sems.at[P_STEPS])
    order = [wv_in, *wq_in]
    for copy in order[:3]:
        copy.start()

    def arrived(i):
        order[i].wait()
        if i + 3 < len(order):
            order[i + 3].start()

    for i in range(PEERS):
        kvt_ref[i * KV_ROWS : (i + 1) * KV_ROWS, :] = g_ref[i, Q_ROWS:, :]
    kv = kvt_ref[:KVL, :].T
    qlat = g_ref[:, :Q_ROWS, :].reshape(QL, TOK).T
    lane = lax.broadcasted_iota(jnp.int32, (TOK, PAD - WIDTH), 1)
    one = jnp.where(lane == 0, 1.0, 0.0).astype(BF16)

    def project_queries(i):
        queries = mm(qlat, wq_ref[:, part(i)]).astype(BF16)
        for j in range(P_HEADS):
            h = i * P_HEADS + j
            q_ref[:, h * PAD : (h + 1) * PAD] = jnp.concatenate(
                [queries[:, j * WIDTH : (j + 1) * WIDTH], one], 1
            )

    k_ref[...] = mm(kv, wk_ref[...]).astype(BF16)
    arrived(0)
    v_ref[...] = mm(kv, wv_ref[...]).astype(BF16)
    for i in range(P_STEPS):
        arrived(1 + i)
        project_queries(i)


def project(g, wq, wk, wv):
    return kernel_call(
        project_kernel,
        "project",
        [
            ((TOK, HEAD_DEV * PAD), BF16),
            ((TOK, HEAD_DEV * NOPE), BF16),
            ((TOK, HEAD_DEV * VDIM), BF16),
            ((KVL + ROPE, TOK), BF16),
            (wv.shape, BF16),
        ],
        g, wq, wk, wv,
        mib=20,
        scratch=[pltpu.VMEM(wq.shape, BF16), pltpu.SemaphoreType.DMA((P_STEPS + 1,))],
        spaces=[None, pltpu.HBM, pltpu.VMEM, pltpu.HBM],
    )


def attend_kernel(lead_ref, kvt_ref, pkvt_ref, q_ref, k_ref, v_ref, do_ref, wk_ref, wv_ref, wq_hbm,
                  out_hbm, ds_ref, po_ref, kp, early_ref, wq_ref,
                  vp, dkp, dvp, out_ref, acc, sems):
    wq_in = pltpu.make_async_copy(wq_hbm, wq_ref, sems.at[O_STEPS])
    wq_in.start()
    wide = HEAD_DEV * VDIM // O_STEPS
    out_copies = [
        pltpu.make_async_copy(
            out_ref.at[:, i * wide : (i + 1) * wide],
            out_hbm.at[:, i * wide : (i + 1) * wide],
            sems.at[i],
        )
        for i in range(O_STEPS)
    ]
    pkv = pkvt_ref[:KVL, :].T

    def expand(h):
        at = slice(h * NOPE, (h + PREV_HEADS) * NOPE)
        kp[:, at] = mm(pkv, wk_ref[:, at]).astype(BF16)
        vp[:, at] = mm(pkv, wv_ref[:, at]).astype(BF16)

    def before(h):
        if h == 0:
            expand(0)
        if h % PREV_HEADS == 0 and h + PREV_HEADS < HEAD_DEV:
            expand(h + PREV_HEADS)

    def after(h):
        if h + 1 not in EARLY_PARTS:
            return
        i = EARLY_PARTS.index(h + 1)
        at = slice(NOPE * (EARLY_PARTS[i - 1] if i else 0), NOPE * (h + 1))
        part = mm(wk_ref[:, at], dkp[:, at], NT) + mm(wv_ref[:, at], dvp[:, at], NT)
        if i:
            part = part + acc[...]
        if h + 1 == HEAD_DEV:
            early_ref[:KVL, :] = part.astype(BF16)
        else:
            acc[...] = part

    ropes_t = jnp.concatenate([pkvt_ref[KVL:, :], kvt_ref[KVL:, :]], 1)
    at_row = lax.broadcasted_iota(jnp.int32, (ROPE, 2 * TOK), 0)
    at_key = lax.broadcasted_iota(jnp.int32, (ROPE, 2 * TOK), 1)
    shut = jnp.where(lead_ref[0] > 0, HIDDEN, 0.0)
    marks_t = jnp.where((at_row == 0) & (at_key < TOK), shut, 0.0).astype(BF16)
    ropes = jnp.concatenate([ropes_t, marks_t], 0).T
    key = lax.broadcasted_iota(jnp.int32, (HALF, HALF), 0)
    query = lax.broadcasted_iota(jnp.int32, (HALF, HALF), 1)
    seen = key <= query
    rope_sum = [None]

    def head(h):
        at = slice(h * NOPE, (h + 1) * NOPE)
        q = q_ref[:, h * PAD : (h + 1) * PAD]
        keys = jnp.concatenate([kp[:, at], k_ref[:, at]], 0)
        vals = jnp.concatenate([vp[:, at], v_ref[:, at]], 0)
        d_out_h = do_ref[:, at]
        d_out_t = d_out_h.T
        scores = mm(jnp.concatenate([keys, ropes], 1), q, NT)
        yield
        s_p = scores[:TOK]
        s_a = jnp.concatenate(
            [
                jnp.where(seen, scores[TOK : TOK + HALF, :HALF], HIDDEN),
                scores[TOK : TOK + HALF, HALF:],
            ],
            1,
        )
        s_b = jnp.where(seen, scores[TOK + HALF :, HALF:], HIDDEN)
        top = jnp.maximum(
            jnp.max(s_p, 0, keepdims=True), jnp.max(s_a, 0, keepdims=True)
        )
        top_b = jnp.maximum(top[:, HALF:], jnp.max(s_b, 0, keepdims=True))
        top = jnp.concatenate([top[:, :HALF], top_b], 1)
        yield
        e_p = jnp.exp2((s_p - top) * EXPONENT)
        e_a = jnp.exp2((s_a - top) * EXPONENT)
        e_b = jnp.exp2((s_b - top_b) * EXPONENT)
        total = jnp.sum(e_p, 0, keepdims=True) + jnp.sum(e_a, 0, keepdims=True)
        total = jnp.concatenate(
            [total[:, :HALF], total[:, HALF:] + jnp.sum(e_b, 0, keepdims=True)], 1
        )
        yield
        inv = 1.0 / total
        invs = inv * SCALE
        none = jnp.zeros((HALF, HALF), BF16)
        probs = jnp.concatenate(
            [
                (e_p * inv).astype(BF16),
                (e_a * inv).astype(BF16),
                jnp.concatenate([none, (e_b * inv[:, HALF:]).astype(BF16)], 1),
            ],
            0,
        )
        yield
        out_t = mm(vals.T, probs).astype(BF16)
        yield
        out_ref[:, at] = out_t.T
        row_dot = jnp.sum(d_out_t.astype(F32) * out_t.astype(F32), 0, keepdims=True)
        yield
        dprob = mm(vals, d_out_t)
        d_p = (e_p * invs * (dprob[:TOK] - row_dot)).astype(BF16)
        d_a = (e_a * invs * (dprob[TOK : TOK + HALF] - row_dot)).astype(BF16)
        d_b = (e_b * invs[:, HALF:] * (dprob[TOK + HALF :, HALF:] - row_dot[:, HALF:])).astype(BF16)
        dscore = jnp.concatenate([d_p, d_a, jnp.concatenate([none, d_b], 1)], 0)
        yield
        ds_ref[h] = dscore
        po_ref[h] = probs[TOK:]
        dk = mm(dscore[:TOK], q)
        dv = mm(probs[:TOK], d_out_h)
        yield
        dk = dk.astype(BF16)
        dkp[:, at] = dk[:, :NOPE]
        dvp[:, at] = dv.astype(BF16)
        rope = dk[:, NOPE:].astype(F32)
        rope_sum[0] = rope if rope_sum[0] is None else rope_sum[0] + rope
        if (h + 1) % (HEAD_DEV // O_STEPS) == 0:
            out_copies[h // (HEAD_DEV // O_STEPS)].start()

    skewed(head, before, after)
    early_ref[KVL:, :] = rope_sum[0].T[:ROPE].astype(BF16)
    for copy in out_copies:
        copy.wait()
    wq_in.wait()


O_STEPS = 4
PREV_HEADS = 2
EARLY_PARTS = (10, 14, 16)


def skewed(make, before, after):
    running = []
    made = done = 0
    while done < HEAD_DEV:
        if made < HEAD_DEV:
            before(made)
            running.append(make(made))
            made += 1
        running = [r for r in running[::-1] if next(r, True) is None][::-1]
        while done < made - len(running):
            after(done)
            done += 1


def attend(lead, kvt, pkvt, q, k, v, d_out, wk, wv, wq):
    return kernel_call(
        attend_kernel,
        "attend",
        [
            ((TOK, HEAD_DEV * VDIM), BF16),
            ((HEAD_DEV, 2 * TOK, TOK), BF16),
            ((HEAD_DEV, TOK, TOK), BF16),
            ((TOK, HEAD_DEV * NOPE), BF16),
            ((KVL + ROPE, TOK), BF16),
            (wq.shape, BF16),
        ],
        lead, kvt, pkvt, q, k, v, d_out, wk, wv, wq,
        mib=20,
        scratch=[pltpu.VMEM((TOK, HEAD_DEV * NOPE), BF16)] * 4
        + [pltpu.VMEM((KVL, TOK), F32), pltpu.SemaphoreType.DMA((O_STEPS + 1,))],
        spaces=[pltpu.SMEM] + [pltpu.VMEM] * 8 + [pltpu.HBM],
        hbm_outs=1,
    )


G_STEPS = PEERS // 2


def gradients_kernel(ds_ref, po_ref, kp_ref, k_ref, kvt_ref, pkvt_ref, q_ref, do_ref,
                     wq_ref, wk_ref, wv_ref, terms_ref, gkv_ref, dqt, dko, dvo):
    ropes_t = jnp.concatenate([pkvt_ref[KVL:, :], kvt_ref[KVL:, :]], 1)
    rope_sum = None
    for h in range(HEAD_DEV):
        at = slice(h * NOPE, (h + 1) * NOPE)
        keys_t = jnp.concatenate([kp_ref[:, at], k_ref[:, at]], 0).T
        dqt[h * WIDTH : (h + 1) * WIDTH, :] = mm(
            jnp.concatenate([keys_t, ropes_t], 0), ds_ref[h]
        ).astype(BF16)
        dk = mm(ds_ref[h, TOK:, :], q_ref[:, h * PAD : (h + 1) * PAD]).astype(BF16)
        dko[:, at] = dk[:, :NOPE]
        dvo[:, at] = mm(po_ref[h], do_ref[:, at]).astype(BF16)
        rope = dk[:, NOPE:].astype(F32)
        rope_sum = rope if rope_sum is None else rope_sum + rope
    gkv_ref[:KVL, :] = mm(wk_ref[...], dko[...], NT) + mm(wv_ref[...], dvo[...], NT)
    gkv_ref[KVL:, :] = rope_sum.T[:ROPE]
    for i in range(G_STEPS):
        part = slice(2 * i * Q_ROWS, 2 * (i + 1) * Q_ROWS)
        rows = mm(wq_ref[part, :], dqt[...]).astype(BF16)
        terms_ref[2 * i, :Q_ROWS, :] = rows[:Q_ROWS]
        terms_ref[2 * i + 1, :Q_ROWS, :] = rows[Q_ROWS:]


def gradients(ds, po, kp, k, kvt, pkvt, q, d_out, wq, wk, wv):
    return kernel_call(
        gradients_kernel,
        "gradients",
        [((PEERS, Q_ROWS, TOK), BF16), ((KVL + ROPE, TOK), F32)],
        ds, po, kp, k, kvt, pkvt, q, d_out, wq, wk, wv,
        scratch=[
            pltpu.VMEM((HEAD_DEV * WIDTH, TOK), BF16),
            pltpu.VMEM((TOK, HEAD_DEV * NOPE), BF16),
            pltpu.VMEM((TOK, HEAD_DEV * VDIM), BF16),
        ],
    )


def total_kernel(terms_ref, q_ref, kv_ref):
    sums = jnp.sum(terms_ref[...].astype(F32), 0)
    q_ref[...] = sums[:Q_ROWS]
    kv_ref[...] = sums[Q_ROWS:]


def total(terms):
    return pl.pallas_call(
        total_kernel,
        out_shape=[
            jax.ShapeDtypeStruct((Q_ROWS, TOK), F32),
            jax.ShapeDtypeStruct((KV_ROWS, TOK), F32),
        ],
        in_specs=[pl.BlockSpec(memory_space=pltpu.VMEM)],
        name="total",
    )(pltpu.with_memory_space_constraint(terms, pltpu.VMEM))


def on_device(q_latent, kv_latent, w_query, w_key, w_value, d_out):
    peers = lax.axis_size("head")
    blocks = lax.axis_size("ctx")
    own = jnp.concatenate([q_latent.T, kv_latent.T], 0)
    copies = jnp.broadcast_to(own, (peers, *own.shape))
    g = lax.all_to_all(copies, "head", 0, 0, tiled=True)
    sent = g[:, Q_ROWS:, :].reshape(KVL + ROPE, TOK)
    pkvt = lax.ppermute(sent, "ctx", [(i, i + 1) for i in range(blocks - 1)])
    q, k, v, kvt, wv_in = project(g, w_query, w_key, w_value)
    lead = (lax.axis_index("ctx") == 0).astype(jnp.int32).reshape(1)
    out, ds, po, kp, early, wq_in = attend(
        lead, kvt, pkvt, q, k, v, d_out, w_key, wv_in, w_query
    )
    later = lax.ppermute(early, "ctx", [(i, i - 1) for i in range(1, blocks)])
    gq, gkv = gradients(
        ds, po, kp, k, kvt, pkvt, q, d_out, wq_in, w_key, wv_in
    )
    gkv = (gkv + later.astype(F32)).astype(BF16)
    terms = jnp.concatenate([gq, gkv.reshape(peers, -1, TOK)], 1)
    terms = lax.all_to_all(terms, "head", 0, 0, tiled=True)
    gq, gkv = total(terms)
    return out, gq.T, gkv.T


def solution(mesh):
    return jax.shard_map(
        on_device,
        mesh=mesh,
        in_specs=(
            P("ctx", "head"),
            P("ctx", "head"),
            P(None, "head"),
            P(None, "head"),
            P(None, "head"),
            P("ctx", "head"),
        ),
        out_specs=(P("ctx", "head"), P("ctx", "head"), P("ctx", "head")),
        check_vma=False,
    )
```

```python
import math

import jax
import jax.numpy as jnp
from jax import lax
from jax.experimental import pallas as pl
from jax.experimental.pallas import tpu as pltpu
from jax.sharding import PartitionSpec as P

QL = 1536
KVL = 512
ROPE = 64
NOPE = 128
VDIM = 128
WIDTH = NOPE + ROPE
PAD = 256
HEAD_DEV = 16
TOK = 256
HALF = TOK // 2
PEERS = 8
Q_ROWS = QL // PEERS
KV_ROWS = (KVL + ROPE) // PEERS
SCALE = WIDTH ** (-0.5)
EXPONENT = SCALE / math.log(2.0)
HIDDEN = -1e30
MIB = 1024 * 1024

NN = (((1,), (0,)), ((), ()))
NT = (((1,), (1,)), ((), ()))
BF16 = jnp.bfloat16
F32 = jnp.float32


def mm(a, b, dims=NN):
    return lax.dot_general(a, b, dims, preferred_element_type=F32)


def kernel_call(body, name, out_shape, *args, mib=16, scratch=(), spaces=None, hbm_outs=0):
    outs = [pltpu.HBM] * hbm_outs + [pltpu.VMEM] * (len(out_shape) - hbm_outs)
    if spaces is None:
        spaces = [pltpu.VMEM] * len(args)
    args = [
        pltpu.with_memory_space_constraint(a, s) if s in (pltpu.VMEM, pltpu.HBM) else a
        for a, s in zip(args, spaces)
    ]
    return pl.pallas_call(
        body,
        in_specs=[pl.BlockSpec(memory_space=s or pltpu.VMEM) for s in spaces],
        out_specs=[pl.BlockSpec(memory_space=s) for s in outs],
        out_shape=[s(shape, dtype) for s, (shape, dtype) in zip(outs, out_shape)],
        scratch_shapes=list(scratch),
        compiler_params=pltpu.CompilerParams(vmem_limit_bytes=mib * MIB),
        name=name,
    )(*args)


P_HEADS = 4
P_STEPS = HEAD_DEV // P_HEADS


def project_kernel(g_ref, kvt_ref, wq_hbm, wk_ref, wv_hbm,
                   q_ref, k_ref, v_ref, wv_ref, wq_ref, sems):
    cols = P_HEADS * WIDTH
    part = lambda i: slice(i * cols, (i + 1) * cols)
    wq_in = [
        pltpu.make_async_copy(wq_hbm.at[:, part(i)], wq_ref.at[:, part(i)], sems.at[i])
        for i in range(P_STEPS)
    ]
    wv_in = pltpu.make_async_copy(wv_hbm, wv_ref, sems.at[P_STEPS])
    order = [wv_in, *wq_in]
    for copy in order[:3]:
        copy.start()

    def arrived(i):
        order[i].wait()
        if i + 3 < len(order):
            order[i + 3].start()

    kv = kvt_ref[:KVL, :].T
    qlat = g_ref[:, :Q_ROWS, :].reshape(QL, TOK).T
    lane = lax.broadcasted_iota(jnp.int32, (TOK, PAD - WIDTH), 1)
    one = jnp.where(lane == 0, 1.0, 0.0).astype(BF16)

    def project_queries(i):
        queries = mm(qlat, wq_ref[:, part(i)]).astype(BF16)
        for j in range(P_HEADS):
            h = i * P_HEADS + j
            q_ref[:, h * PAD : (h + 1) * PAD] = jnp.concatenate(
                [queries[:, j * WIDTH : (j + 1) * WIDTH], one], 1
            )

    k_ref[...] = mm(kv, wk_ref[...]).astype(BF16)
    arrived(0)
    v_ref[...] = mm(kv, wv_ref[...]).astype(BF16)
    for i in range(P_STEPS):
        arrived(1 + i)
        project_queries(i)


def project(g, kvt, wq, wk, wv):
    return kernel_call(
        project_kernel,
        "project",
        [
            ((TOK, HEAD_DEV * PAD), BF16),
            ((TOK, HEAD_DEV * NOPE), BF16),
            ((TOK, HEAD_DEV * VDIM), BF16),
            (wv.shape, BF16),
        ],
        g, kvt, wq, wk, wv,
        mib=20,
        scratch=[pltpu.VMEM(wq.shape, BF16), pltpu.SemaphoreType.DMA((P_STEPS + 1,))],
        spaces=[None, pltpu.VMEM, pltpu.HBM, pltpu.VMEM, pltpu.HBM],
    )


def attend_kernel(lead_ref, kvt_ref, pkvt_ref, q_ref, k_ref, v_ref, do_ref, wk_ref, wv_ref, wq_hbm,
                  out_hbm, ds_ref, po_ref, kp, early_ref, wq_ref,
                  vp, dkp, dvp, out_ref, acc, sems):
    wq_in = pltpu.make_async_copy(wq_hbm, wq_ref, sems.at[O_STEPS])
    wq_in.start()
    wide = HEAD_DEV * VDIM // O_STEPS
    out_copies = [
        pltpu.make_async_copy(
            out_ref.at[:, i * wide : (i + 1) * wide],
            out_hbm.at[:, i * wide : (i + 1) * wide],
            sems.at[i],
        )
        for i in range(O_STEPS)
    ]
    pkv = pkvt_ref[:KVL, :].T

    def expand(h):
        at = slice(h * NOPE, (h + PREV_HEADS) * NOPE)
        kp[:, at] = mm(pkv, wk_ref[:, at]).astype(BF16)
        vp[:, at] = mm(pkv, wv_ref[:, at]).astype(BF16)

    def before(h):
        if h == 0:
            expand(0)
        if h % PREV_HEADS == 0 and h + PREV_HEADS < HEAD_DEV:
            expand(h + PREV_HEADS)

    def after(h):
        if h + 1 not in EARLY_PARTS:
            return
        i = EARLY_PARTS.index(h + 1)
        at = slice(NOPE * (EARLY_PARTS[i - 1] if i else 0), NOPE * (h + 1))
        part = mm(wk_ref[:, at], dkp[:, at], NT) + mm(wv_ref[:, at], dvp[:, at], NT)
        if i:
            part = part + acc[...]
        if h + 1 == HEAD_DEV:
            early_ref[:KVL, :] = part.astype(BF16)
        else:
            acc[...] = part

    ropes_t = jnp.concatenate([pkvt_ref[KVL:, :], kvt_ref[KVL:, :]], 1)
    at_row = lax.broadcasted_iota(jnp.int32, (ROPE, 2 * TOK), 0)
    at_key = lax.broadcasted_iota(jnp.int32, (ROPE, 2 * TOK), 1)
    shut = jnp.where(lead_ref[0] > 0, HIDDEN, 0.0)
    marks_t = jnp.where((at_row == 0) & (at_key < TOK), shut, 0.0).astype(BF16)
    ropes = jnp.concatenate([ropes_t, marks_t], 0).T
    key = lax.broadcasted_iota(jnp.int32, (HALF, HALF), 0)
    query = lax.broadcasted_iota(jnp.int32, (HALF, HALF), 1)
    seen = key <= query
    rope_sum = [None]

    def head(h):
        at = slice(h * NOPE, (h + 1) * NOPE)
        q = q_ref[:, h * PAD : (h + 1) * PAD]
        keys = jnp.concatenate([kp[:, at], k_ref[:, at]], 0)
        vals = jnp.concatenate([vp[:, at], v_ref[:, at]], 0)
        d_out_h = do_ref[:, at]
        d_out_t = d_out_h.T
        scores = mm(jnp.concatenate([keys, ropes], 1), q, NT)
        yield
        s_p = scores[:TOK]
        s_a = jnp.concatenate(
            [
                jnp.where(seen, scores[TOK : TOK + HALF, :HALF], HIDDEN),
                scores[TOK : TOK + HALF, HALF:],
            ],
            1,
        )
        s_b = jnp.where(seen, scores[TOK + HALF :, HALF:], HIDDEN)
        top = jnp.maximum(
            jnp.max(s_p, 0, keepdims=True), jnp.max(s_a, 0, keepdims=True)
        )
        top_b = jnp.maximum(top[:, HALF:], jnp.max(s_b, 0, keepdims=True))
        top = jnp.concatenate([top[:, :HALF], top_b], 1)
        yield
        e_p = jnp.exp2((s_p - top) * EXPONENT)
        e_a = jnp.exp2((s_a - top) * EXPONENT)
        e_b = jnp.exp2((s_b - top_b) * EXPONENT)
        total = jnp.sum(e_p, 0, keepdims=True) + jnp.sum(e_a, 0, keepdims=True)
        total = jnp.concatenate(
            [total[:, :HALF], total[:, HALF:] + jnp.sum(e_b, 0, keepdims=True)], 1
        )
        yield
        inv = 1.0 / total
        invs = inv * SCALE
        none = jnp.zeros((HALF, HALF), BF16)
        probs = jnp.concatenate(
            [
                (e_p * inv).astype(BF16),
                (e_a * inv).astype(BF16),
                jnp.concatenate([none, (e_b * inv[:, HALF:]).astype(BF16)], 1),
            ],
            0,
        )
        yield
        out_t = mm(vals.T, probs).astype(BF16)
        yield
        out_ref[:, at] = out_t.T
        row_dot = jnp.sum(d_out_t.astype(F32) * out_t.astype(F32), 0, keepdims=True)
        yield
        dprob = mm(vals, d_out_t)
        d_p = (e_p * invs * (dprob[:TOK] - row_dot)).astype(BF16)
        d_a = (e_a * invs * (dprob[TOK : TOK + HALF] - row_dot)).astype(BF16)
        d_b = (e_b * invs[:, HALF:] * (dprob[TOK + HALF :, HALF:] - row_dot[:, HALF:])).astype(BF16)
        dscore = jnp.concatenate([d_p, d_a, jnp.concatenate([none, d_b], 1)], 0)
        yield
        ds_ref[h] = dscore
        po_ref[h] = probs[TOK:]
        dk = mm(dscore[:TOK], q)
        dv = mm(probs[:TOK], d_out_h)
        yield
        dk = dk.astype(BF16)
        dkp[:, at] = dk[:, :NOPE]
        dvp[:, at] = dv.astype(BF16)
        rope = dk[:, NOPE:].astype(F32)
        rope_sum[0] = rope if rope_sum[0] is None else rope_sum[0] + rope
        if (h + 1) % (HEAD_DEV // O_STEPS) == 0:
            out_copies[h // (HEAD_DEV // O_STEPS)].start()

    skewed(head, before, after)
    early_ref[KVL:, :] = rope_sum[0].T[:ROPE].astype(BF16)
    for copy in out_copies:
        copy.wait()
    wq_in.wait()


O_STEPS = 4
PREV_HEADS = 2
EARLY_PARTS = (10, 14, 16)


def skewed(make, before, after):
    running = []
    made = done = 0
    while done < HEAD_DEV:
        if made < HEAD_DEV:
            before(made)
            running.append(make(made))
            made += 1
        running = [r for r in running[::-1] if next(r, True) is None][::-1]
        while done < made - len(running):
            after(done)
            done += 1


def attend(lead, kvt, pkvt, q, k, v, d_out, wk, wv, wq):
    return kernel_call(
        attend_kernel,
        "attend",
        [
            ((TOK, HEAD_DEV * VDIM), BF16),
            ((HEAD_DEV, 2 * TOK, TOK), BF16),
            ((HEAD_DEV, TOK, TOK), BF16),
            ((TOK, HEAD_DEV * NOPE), BF16),
            ((KVL + ROPE, TOK), BF16),
            (wq.shape, BF16),
        ],
        lead, kvt, pkvt, q, k, v, d_out, wk, wv, wq,
        mib=20,
        scratch=[pltpu.VMEM((TOK, HEAD_DEV * NOPE), BF16)] * 4
        + [pltpu.VMEM((KVL, TOK), F32), pltpu.SemaphoreType.DMA((O_STEPS + 1,))],
        spaces=[pltpu.SMEM] + [pltpu.VMEM] * 8 + [pltpu.HBM],
        hbm_outs=1,
    )


G_STEPS = PEERS // 2


def gradients_kernel(ds_ref, po_ref, kp_ref, k_ref, kvt_ref, pkvt_ref, q_ref, do_ref,
                     wq_ref, wk_ref, wv_ref, terms_ref, gkv_ref, dqt, dko, dvo):
    ropes_t = jnp.concatenate([pkvt_ref[KVL:, :], kvt_ref[KVL:, :]], 1)
    rope_sum = None
    for h in range(HEAD_DEV):
        at = slice(h * NOPE, (h + 1) * NOPE)
        keys_t = jnp.concatenate([kp_ref[:, at], k_ref[:, at]], 0).T
        dqt[h * WIDTH : (h + 1) * WIDTH, :] = mm(
            jnp.concatenate([keys_t, ropes_t], 0), ds_ref[h]
        ).astype(BF16)
        dk = mm(ds_ref[h, TOK:, :], q_ref[:, h * PAD : (h + 1) * PAD]).astype(BF16)
        dko[:, at] = dk[:, :NOPE]
        dvo[:, at] = mm(po_ref[h], do_ref[:, at]).astype(BF16)
        rope = dk[:, NOPE:].astype(F32)
        rope_sum = rope if rope_sum is None else rope_sum + rope
    gkv_ref[:KVL, :] = mm(wk_ref[...], dko[...], NT) + mm(wv_ref[...], dvo[...], NT)
    gkv_ref[KVL:, :] = rope_sum.T[:ROPE]
    for i in range(G_STEPS):
        part = slice(2 * i * Q_ROWS, 2 * (i + 1) * Q_ROWS)
        rows = mm(wq_ref[part, :], dqt[...]).astype(BF16)
        terms_ref[2 * i, :Q_ROWS, :] = rows[:Q_ROWS]
        terms_ref[2 * i + 1, :Q_ROWS, :] = rows[Q_ROWS:]


def gradients(ds, po, kp, k, kvt, pkvt, q, d_out, wq, wk, wv):
    return kernel_call(
        gradients_kernel,
        "gradients",
        [((PEERS, Q_ROWS, TOK), BF16), ((KVL + ROPE, TOK), F32)],
        ds, po, kp, k, kvt, pkvt, q, d_out, wq, wk, wv,
        scratch=[
            pltpu.VMEM((HEAD_DEV * WIDTH, TOK), BF16),
            pltpu.VMEM((TOK, HEAD_DEV * NOPE), BF16),
            pltpu.VMEM((TOK, HEAD_DEV * VDIM), BF16),
        ],
    )


def total_kernel(terms_ref, q_ref, kv_ref):
    sums = jnp.sum(terms_ref[...].astype(F32), 0)
    q_ref[...] = sums[:Q_ROWS]
    kv_ref[...] = sums[Q_ROWS:]


def total(terms):
    return pl.pallas_call(
        total_kernel,
        out_shape=[
            jax.ShapeDtypeStruct((Q_ROWS, TOK), F32),
            jax.ShapeDtypeStruct((KV_ROWS, TOK), F32),
        ],
        in_specs=[pl.BlockSpec(memory_space=pltpu.VMEM)],
        name="total",
    )(pltpu.with_memory_space_constraint(terms, pltpu.VMEM))


def on_device(q_latent, kv_latent, w_query, w_key, w_value, d_out):
    peers = lax.axis_size("head")
    blocks = lax.axis_size("ctx")
    own = jnp.concatenate([q_latent.T, kv_latent.T], 0)
    copies = jnp.broadcast_to(own, (peers, *own.shape))
    g = lax.all_to_all(copies, "head", 0, 0, tiled=True)
    kvt = g[:, Q_ROWS:, :].reshape(KVL + ROPE, TOK)
    pkvt = lax.ppermute(kvt, "ctx", [(i, i + 1) for i in range(blocks - 1)])
    q, k, v, wv_in = project(g, kvt, w_query, w_key, w_value)
    lead = (lax.axis_index("ctx") == 0).astype(jnp.int32).reshape(1)
    out, ds, po, kp, early, wq_in = attend(
        lead, kvt, pkvt, q, k, v, d_out, w_key, wv_in, w_query
    )
    later = lax.ppermute(early, "ctx", [(i, i - 1) for i in range(1, blocks)])
    gq, gkv = gradients(
        ds, po, kp, k, kvt, pkvt, q, d_out, wq_in, w_key, wv_in
    )
    gkv = (gkv + later.astype(F32)).astype(BF16)
    terms = jnp.concatenate([gq, gkv.reshape(peers, -1, TOK)], 1)
    terms = lax.all_to_all(terms, "head", 0, 0, tiled=True)
    gq, gkv = total(terms)
    return out, gq.T, gkv.T


def solution(mesh):
    return jax.shard_map(
        on_device,
        mesh=mesh,
        in_specs=(
            P("ctx", "head"),
            P("ctx", "head"),
            P(None, "head"),
            P(None, "head"),
            P(None, "head"),
            P("ctx", "head"),
        ),
        out_specs=(P("ctx", "head"), P("ctx", "head"), P("ctx", "head")),
        check_vma=False,
    )
```

```python
import math

import jax
import jax.numpy as jnp
from jax import lax
from jax.experimental import pallas as pl
from jax.experimental.pallas import tpu as pltpu
from jax.sharding import PartitionSpec as P

QL = 1536
KVL = 512
ROPE = 64
NOPE = 128
VDIM = 128
WIDTH = NOPE + ROPE
PAD = 256
HEAD_DEV = 16
TOK = 256
HALF = TOK // 2
PEERS = 8
Q_ROWS = QL // PEERS
KV_ROWS = (KVL + ROPE) // PEERS
SCALE = WIDTH ** (-0.5)
EXPONENT = SCALE / math.log(2.0)
HIDDEN = -1e30
MIB = 1024 * 1024

NN = (((1,), (0,)), ((), ()))
NT = (((1,), (1,)), ((), ()))
BF16 = jnp.bfloat16
F32 = jnp.float32


def mm(a, b, dims=NN):
    return lax.dot_general(a, b, dims, preferred_element_type=F32)


def kernel_call(body, name, out_shape, *args, mib=16, scratch=(), spaces=None, hbm_outs=0):
    outs = [pltpu.HBM] * hbm_outs + [pltpu.VMEM] * (len(out_shape) - hbm_outs)
    if spaces is None:
        spaces = [pltpu.VMEM] * len(args)
    args = [
        pltpu.with_memory_space_constraint(a, s) if s in (pltpu.VMEM, pltpu.HBM) else a
        for a, s in zip(args, spaces)
    ]
    return pl.pallas_call(
        body,
        in_specs=[pl.BlockSpec(memory_space=s or pltpu.VMEM) for s in spaces],
        out_specs=[pl.BlockSpec(memory_space=s) for s in outs],
        out_shape=[s(shape, dtype) for s, (shape, dtype) in zip(outs, out_shape)],
        scratch_shapes=list(scratch),
        compiler_params=pltpu.CompilerParams(vmem_limit_bytes=mib * MIB),
        name=name,
    )(*args)


P_HEADS = 4
P_STEPS = HEAD_DEV // P_HEADS


def project_kernel(g_ref, wq_hbm, wk_hbm, wv_hbm,
                   q_ref, k_ref, v_ref, kvt_ref, wk_ref, wv_ref, wq_ref, sems):
    cols = P_HEADS * WIDTH
    part = lambda i: slice(i * cols, (i + 1) * cols)
    wq_in = [
        pltpu.make_async_copy(wq_hbm.at[:, part(i)], wq_ref.at[:, part(i)], sems.at[i])
        for i in range(P_STEPS)
    ]
    wv_in = pltpu.make_async_copy(wv_hbm, wv_ref, sems.at[P_STEPS])
    wk_in = pltpu.make_async_copy(wk_hbm, wk_ref, sems.at[P_STEPS + 1])
    order = [wk_in, wv_in, *wq_in]
    for copy in order[:3]:
        copy.start()

    def arrived(i):
        order[i].wait()
        if i + 3 < len(order):
            order[i + 3].start()

    for i in range(PEERS):
        kvt_ref[i * KV_ROWS : (i + 1) * KV_ROWS, :] = g_ref[i, Q_ROWS:, :]
    kv = kvt_ref[:KVL, :].T
    qlat = g_ref[:, :Q_ROWS, :].reshape(QL, TOK).T
    lane = lax.broadcasted_iota(jnp.int32, (TOK, PAD - WIDTH), 1)
    one = jnp.where(lane == 0, 1.0, 0.0).astype(BF16)

    def project_queries(i):
        queries = mm(qlat, wq_ref[:, part(i)]).astype(BF16)
        for j in range(P_HEADS):
            h = i * P_HEADS + j
            q_ref[:, h * PAD : (h + 1) * PAD] = jnp.concatenate(
                [queries[:, j * WIDTH : (j + 1) * WIDTH], one], 1
            )

    arrived(0)
    k_ref[...] = mm(kv, wk_ref[...]).astype(BF16)
    arrived(1)
    v_ref[...] = mm(kv, wv_ref[...]).astype(BF16)
    for i in range(P_STEPS):
        arrived(2 + i)
        project_queries(i)


def project(g, wq, wk, wv):
    return kernel_call(
        project_kernel,
        "project",
        [
            ((TOK, HEAD_DEV * PAD), BF16),
            ((TOK, HEAD_DEV * NOPE), BF16),
            ((TOK, HEAD_DEV * VDIM), BF16),
            ((KVL + ROPE, TOK), BF16),
            (wk.shape, BF16),
            (wv.shape, BF16),
        ],
        g, wq, wk, wv,
        mib=20,
        scratch=[pltpu.VMEM(wq.shape, BF16), pltpu.SemaphoreType.DMA((P_STEPS + 2,))],
        spaces=[None] + [pltpu.HBM] * 3,
    )


def attend_kernel(lead_ref, kvt_ref, pkvt_ref, q_ref, k_ref, v_ref, do_ref, wk_ref, wv_ref, wq_hbm,
                  out_hbm, ds_ref, po_ref, kp, early_ref, wq_ref,
                  vp, dkp, dvp, out_ref, acc, sems):
    wq_in = pltpu.make_async_copy(wq_hbm, wq_ref, sems.at[O_STEPS])
    wq_in.start()
    wide = HEAD_DEV * VDIM // O_STEPS
    out_copies = [
        pltpu.make_async_copy(
            out_ref.at[:, i * wide : (i + 1) * wide],
            out_hbm.at[:, i * wide : (i + 1) * wide],
            sems.at[i],
        )
        for i in range(O_STEPS)
    ]
    pkv = pkvt_ref[:KVL, :].T

    def expand(h):
        at = slice(h * NOPE, (h + PREV_HEADS) * NOPE)
        kp[:, at] = mm(pkv, wk_ref[:, at]).astype(BF16)
        vp[:, at] = mm(pkv, wv_ref[:, at]).astype(BF16)

    def before(h):
        if h == 0:
            expand(0)
        if h % PREV_HEADS == 0 and h + PREV_HEADS < HEAD_DEV:
            expand(h + PREV_HEADS)

    def after(h):
        if h + 1 not in EARLY_PARTS:
            return
        i = EARLY_PARTS.index(h + 1)
        at = slice(NOPE * (EARLY_PARTS[i - 1] if i else 0), NOPE * (h + 1))
        part = mm(wk_ref[:, at], dkp[:, at], NT) + mm(wv_ref[:, at], dvp[:, at], NT)
        if i:
            part = part + acc[...]
        if h + 1 == HEAD_DEV:
            early_ref[:KVL, :] = part.astype(BF16)
        else:
            acc[...] = part

    ropes_t = jnp.concatenate([pkvt_ref[KVL:, :], kvt_ref[KVL:, :]], 1)
    at_row = lax.broadcasted_iota(jnp.int32, (ROPE, 2 * TOK), 0)
    at_key = lax.broadcasted_iota(jnp.int32, (ROPE, 2 * TOK), 1)
    shut = jnp.where(lead_ref[0] > 0, HIDDEN, 0.0)
    marks_t = jnp.where((at_row == 0) & (at_key < TOK), shut, 0.0).astype(BF16)
    ropes = jnp.concatenate([ropes_t, marks_t], 0).T
    key = lax.broadcasted_iota(jnp.int32, (HALF, HALF), 0)
    query = lax.broadcasted_iota(jnp.int32, (HALF, HALF), 1)
    seen = key <= query
    rope_sum = [None]

    def head(h):
        at = slice(h * NOPE, (h + 1) * NOPE)
        q = q_ref[:, h * PAD : (h + 1) * PAD]
        keys = jnp.concatenate([kp[:, at], k_ref[:, at]], 0)
        vals = jnp.concatenate([vp[:, at], v_ref[:, at]], 0)
        d_out_h = do_ref[:, at]
        d_out_t = d_out_h.T
        scores = mm(jnp.concatenate([keys, ropes], 1), q, NT)
        yield
        s_p = scores[:TOK]
        s_a = jnp.concatenate(
            [
                jnp.where(seen, scores[TOK : TOK + HALF, :HALF], HIDDEN),
                scores[TOK : TOK + HALF, HALF:],
            ],
            1,
        )
        s_b = jnp.where(seen, scores[TOK + HALF :, HALF:], HIDDEN)
        top = jnp.maximum(
            jnp.max(s_p, 0, keepdims=True), jnp.max(s_a, 0, keepdims=True)
        )
        top_b = jnp.maximum(top[:, HALF:], jnp.max(s_b, 0, keepdims=True))
        top = jnp.concatenate([top[:, :HALF], top_b], 1)
        yield
        e_p = jnp.exp2((s_p - top) * EXPONENT)
        e_a = jnp.exp2((s_a - top) * EXPONENT)
        e_b = jnp.exp2((s_b - top_b) * EXPONENT)
        total = jnp.sum(e_p, 0, keepdims=True) + jnp.sum(e_a, 0, keepdims=True)
        total = jnp.concatenate(
            [total[:, :HALF], total[:, HALF:] + jnp.sum(e_b, 0, keepdims=True)], 1
        )
        yield
        inv = 1.0 / total
        invs = inv * SCALE
        none = jnp.zeros((HALF, HALF), BF16)
        probs = jnp.concatenate(
            [
                (e_p * inv).astype(BF16),
                (e_a * inv).astype(BF16),
                jnp.concatenate([none, (e_b * inv[:, HALF:]).astype(BF16)], 1),
            ],
            0,
        )
        yield
        out_t = mm(vals.T, probs).astype(BF16)
        yield
        out_ref[:, at] = out_t.T
        row_dot = jnp.sum(d_out_t.astype(F32) * out_t.astype(F32), 0, keepdims=True)
        yield
        dprob = mm(vals, d_out_t)
        d_p = (e_p * invs * (dprob[:TOK] - row_dot)).astype(BF16)
        d_a = (e_a * invs * (dprob[TOK : TOK + HALF] - row_dot)).astype(BF16)
        d_b = (e_b * invs[:, HALF:] * (dprob[TOK + HALF :, HALF:] - row_dot[:, HALF:])).astype(BF16)
        dscore = jnp.concatenate([d_p, d_a, jnp.concatenate([none, d_b], 1)], 0)
        yield
        ds_ref[h] = dscore
        po_ref[h] = probs[TOK:]
        dk = mm(dscore[:TOK], q)
        dv = mm(probs[:TOK], d_out_h)
        yield
        dk = dk.astype(BF16)
        dkp[:, at] = dk[:, :NOPE]
        dvp[:, at] = dv.astype(BF16)
        rope = dk[:, NOPE:].astype(F32)
        rope_sum[0] = rope if rope_sum[0] is None else rope_sum[0] + rope
        if (h + 1) % (HEAD_DEV // O_STEPS) == 0:
            out_copies[h // (HEAD_DEV // O_STEPS)].start()

    skewed(head, before, after)
    early_ref[KVL:, :] = rope_sum[0].T[:ROPE].astype(BF16)
    for copy in out_copies:
        copy.wait()
    wq_in.wait()


O_STEPS = 4
PREV_HEADS = 2
EARLY_PARTS = (6, 10, 14, 16)


def skewed(make, before, after):
    running = []
    made = done = 0
    while done < HEAD_DEV:
        if made < HEAD_DEV:
            before(made)
            running.append(make(made))
            made += 1
        running = [r for r in running[::-1] if next(r, True) is None][::-1]
        while done < made - len(running):
            after(done)
            done += 1


def attend(lead, kvt, pkvt, q, k, v, d_out, wk, wv, wq):
    return kernel_call(
        attend_kernel,
        "attend",
        [
            ((TOK, HEAD_DEV * VDIM), BF16),
            ((HEAD_DEV, 2 * TOK, TOK), BF16),
            ((HEAD_DEV, TOK, TOK), BF16),
            ((TOK, HEAD_DEV * NOPE), BF16),
            ((KVL + ROPE, TOK), BF16),
            (wq.shape, BF16),
        ],
        lead, kvt, pkvt, q, k, v, d_out, wk, wv, wq,
        mib=20,
        scratch=[pltpu.VMEM((TOK, HEAD_DEV * NOPE), BF16)] * 4
        + [pltpu.VMEM((KVL, TOK), F32), pltpu.SemaphoreType.DMA((O_STEPS + 1,))],
        spaces=[pltpu.SMEM] + [pltpu.VMEM] * 8 + [pltpu.HBM],
        hbm_outs=1,
    )


G_STEPS = PEERS // 2


def gradients_kernel(ds_ref, po_ref, kp_ref, k_ref, kvt_ref, pkvt_ref, q_ref, do_ref,
                     wq_ref, wk_ref, wv_ref, terms_ref, gkv_ref, dqt, dko, dvo):
    ropes_t = jnp.concatenate([pkvt_ref[KVL:, :], kvt_ref[KVL:, :]], 1)
    rope_sum = None
    for h in range(HEAD_DEV):
        at = slice(h * NOPE, (h + 1) * NOPE)
        keys_t = jnp.concatenate([kp_ref[:, at], k_ref[:, at]], 0).T
        dqt[h * WIDTH : (h + 1) * WIDTH, :] = mm(
            jnp.concatenate([keys_t, ropes_t], 0), ds_ref[h]
        ).astype(BF16)
        dk = mm(ds_ref[h, TOK:, :], q_ref[:, h * PAD : (h + 1) * PAD]).astype(BF16)
        dko[:, at] = dk[:, :NOPE]
        dvo[:, at] = mm(po_ref[h], do_ref[:, at]).astype(BF16)
        rope = dk[:, NOPE:].astype(F32)
        rope_sum = rope if rope_sum is None else rope_sum + rope
    gkv_ref[:KVL, :] = mm(wk_ref[...], dko[...], NT) + mm(wv_ref[...], dvo[...], NT)
    gkv_ref[KVL:, :] = rope_sum.T[:ROPE]
    for i in range(G_STEPS):
        part = slice(2 * i * Q_ROWS, 2 * (i + 1) * Q_ROWS)
        rows = mm(wq_ref[part, :], dqt[...]).astype(BF16)
        terms_ref[2 * i, :Q_ROWS, :] = rows[:Q_ROWS]
        terms_ref[2 * i + 1, :Q_ROWS, :] = rows[Q_ROWS:]


def gradients(ds, po, kp, k, kvt, pkvt, q, d_out, wq, wk, wv):
    return kernel_call(
        gradients_kernel,
        "gradients",
        [((PEERS, Q_ROWS, TOK), BF16), ((KVL + ROPE, TOK), F32)],
        ds, po, kp, k, kvt, pkvt, q, d_out, wq, wk, wv,
        scratch=[
            pltpu.VMEM((HEAD_DEV * WIDTH, TOK), BF16),
            pltpu.VMEM((TOK, HEAD_DEV * NOPE), BF16),
            pltpu.VMEM((TOK, HEAD_DEV * VDIM), BF16),
        ],
    )


def total_kernel(terms_ref, q_ref, kv_ref):
    sums = jnp.sum(terms_ref[...].astype(F32), 0)
    q_ref[...] = sums[:Q_ROWS]
    kv_ref[...] = sums[Q_ROWS:]


def total(terms):
    return pl.pallas_call(
        total_kernel,
        out_shape=[
            jax.ShapeDtypeStruct((Q_ROWS, TOK), F32),
            jax.ShapeDtypeStruct((KV_ROWS, TOK), F32),
        ],
        in_specs=[pl.BlockSpec(memory_space=pltpu.VMEM)],
        name="total",
    )(pltpu.with_memory_space_constraint(terms, pltpu.VMEM))


def on_device(q_latent, kv_latent, w_query, w_key, w_value, d_out):
    peers = lax.axis_size("head")
    blocks = lax.axis_size("ctx")
    own = jnp.concatenate([q_latent.T, kv_latent.T], 0)
    copies = jnp.broadcast_to(own, (peers, *own.shape))
    g = lax.all_to_all(copies, "head", 0, 0, tiled=True)
    sent = g[:, Q_ROWS:, :].reshape(KVL + ROPE, TOK)
    pkvt = lax.ppermute(sent, "ctx", [(i, i + 1) for i in range(blocks - 1)])
    q, k, v, kvt, wk_in, wv_in = project(g, w_query, w_key, w_value)
    lead = (lax.axis_index("ctx") == 0).astype(jnp.int32).reshape(1)
    out, ds, po, kp, early, wq_in = attend(
        lead, kvt, pkvt, q, k, v, d_out, wk_in, wv_in, w_query
    )
    later = lax.ppermute(early, "ctx", [(i, i - 1) for i in range(1, blocks)])
    gq, gkv = gradients(
        ds, po, kp, k, kvt, pkvt, q, d_out, wq_in, wk_in, wv_in
    )
    gkv = (gkv + later.astype(F32)).astype(BF16)
    terms = jnp.concatenate([gq, gkv.reshape(peers, -1, TOK)], 1)
    terms = lax.all_to_all(terms, "head", 0, 0, tiled=True)
    gq, gkv = total(terms)
    return out, gq.T, gkv.T


def solution(mesh):
    return jax.shard_map(
        on_device,
        mesh=mesh,
        in_specs=(
            P("ctx", "head"),
            P("ctx", "head"),
            P(None, "head"),
            P(None, "head"),
            P(None, "head"),
            P("ctx", "head"),
        ),
        out_specs=(P("ctx", "head"), P("ctx", "head"), P("ctx", "head")),
        check_vma=False,
    )
```
